32 devices in a mesh: rep: 2 (over y), sample: 4 (over z), head: 4 (over x, core).
Axes of the slice: x: 2, y: 2, z: 4, core: 2. Of those that a mesh axis runs over, the one named last changes fastest.
Arguments:
- x_pre: bfloat16 [8, 128, 8192], P(('rep', 'sample'), None, 'head'), parts along dimension 0, may hold values from -120 to 120
- z_pre: bfloat16 [8, 128, 8192], P(('rep', 'sample'), None, 'head'), parts along dimension 0, may hold values from -6 to 6
- b_pre: bfloat16 [8, 128, 512], P(('rep', 'sample')), parts along dimension 0, may hold values from -1.796875 to 1.796875
- c_pre: bfloat16 [8, 128, 512], P(('rep', 'sample')), parts along dimension 0, may hold values from -0.5390625 to 0.5390625
- dt_pre: float32 [8, 128, 128], P(('rep', 'sample'), None, 'head'), parts along dimension 0, may hold values from -1.5 to 7.5
- lengths: int32 [8], P(('rep', 'sample')), parts along dimension 0, may hold values from 64 to 128, as said below
- init_state: float32 [8, 128, 8192], P(('rep', 'sample'), None, 'head'), parts along dimension 0, may hold values from -6 to 6
- a_rates: float32 [128], P('head'), may hold values from 0.005 to 0.3
- dt_bias: float32 [128], P('head'), may hold values from -2 to -1
- skip_scale: float32 [128], P('head'), may hold values from 0.5 to 2
- norm_gain: float32 [8192], P('head'), may hold values from 0.5 to 1.5
- x_dec: bfloat16 [8, 4, 8192], P(('rep', 'sample'), None, 'head'), parts along dimension 0, may hold values from -120 to 120
- z_dec: bfloat16 [8, 4, 8192], P(('rep', 'sample'), None, 'head'), parts along dimension 0, may hold values from -6 to 6
- b_dec: bfloat16 [8, 4, 512], P(('rep', 'sample')), parts along dimension 0, may hold values from -6 to 6
- c_dec: bfloat16 [8, 4, 512], P(('rep', 'sample')), parts along dimension 0, may hold values from -0.5390625 to 0.5390625
- dt_dec: float32 [8, 4, 128], P(('rep', 'sample'), None, 'head'), parts along dimension 0, may hold values from -3 to 3
Outputs:
- out_pre: bfloat16 [8, 128, 8192], P(('rep', 'sample'), None, 'head'), parts along dimension 0
- final_state: bfloat16 [8, 128, 8192], P(('rep', 'sample'), None, 'head'), parts along dimension 0
- out_dec: bfloat16 [8, 4, 8192], P(('rep', 'sample'), None, 'head'), parts along dimension 0
The draws below stay inside these ranges and needn't reach their ends.
There are 2 independent parts, one for each index of `rep`. The reference program is written for one: setup_inputs(seed, part) draws one part's arguments, and reference() takes and returns one part's arrays. A program takes and returns all parts, laid end to end along the dimension named above; an argument that names none is the same for every part. Nothing has to cross between parts.
Inputs may be any that keep to these rules, and one draw needn't show every extreme that they name: Each prompt's valid tokens are the first lengths[p] of its 128 positions; some prompt uses all 128.
All inputs are finite; a program needn't handle non-finite values.
Results may differ from the reference program's by a relative error of at most 0.006.
Values may be sent and summed in bfloat16 or wider, within the bound.
No kernel may reach another device: no remote copies, remote signals or barrier semaphores. Data moves between devices by JAX's collectives and lax.ppermute only.
A program may use at most 64 MiB of HBM per device.

```python
import jax
import jax.numpy as jnp
from jax import lax

H = 128
P_SIZE = 64
N = 128
G = 4
BLOCK = 128
TAIL_TOKENS = 128
PROMPT_TOTAL = 4
SLOTS = 4
INNER = 8192


def rising_channels(key, shape):
    split_random_keys = jax.random.split(key, 3)
    base_draw = jnp.clip(jax.random.normal(split_random_keys[0], shape, jnp.float32), -4.0, 4.0)
    row_scale = jnp.exp(jax.random.uniform(split_random_keys[1], shape[:-1] + (1,), jnp.float32, jnp.log(0.3), jnp.log(3.0)))
    head_ids = (jnp.arange(shape[-1]) // P_SIZE).astype(jnp.float32)
    rise_factor = jnp.sqrt(1.0 + 2.0 * head_ids / (H - 1))
    col_scale = jnp.exp(jax.random.uniform(split_random_keys[2], (shape[-1],), jnp.float32, jnp.log(0.3), jnp.log(3.0))) * rise_factor
    return (base_draw * row_scale * col_scale).astype(jnp.bfloat16)


def draw_x_pre(key, part):
    return rising_channels(jax.random.fold_in(key, 11), (PROMPT_TOTAL, TAIL_TOKENS, H * P_SIZE))


def draw_x_dec(key, part):
    return rising_channels(jax.random.fold_in(key, 12), (SLOTS, PROMPT_TOTAL, H * P_SIZE))


def draw_dt_pre(key, part):
    split_random_keys = jax.random.split(jax.random.fold_in(key, 13), 2)
    random_jitter = jnp.clip(0.5 * jax.random.normal(split_random_keys[0], (PROMPT_TOTAL, TAIL_TOKENS, H), jnp.float32), -1.5, 1.5)
    spike_position = jax.random.randint(split_random_keys[1], (PROMPT_TOTAL, 3), 0, TAIL_TOKENS // 2)
    spike_events = jnp.any(jnp.arange(TAIL_TOKENS)[None, None, :] == spike_position[:, :, None], axis=1).astype(jnp.float32)
    return random_jitter + 6.0 * spike_events[:, :, None]


def draw_a_rates(key, part):
    lower, upper = (0.02, 0.3)
    return jnp.exp(jax.random.uniform(jax.random.fold_in(key, 14), (H,), jnp.float32, jnp.log(lower), jnp.log(upper)))


def draw_lengths(key, part):
    split_random_keys = jax.random.split(jax.random.fold_in(key, 15), 2)
    drawn = jax.random.randint(split_random_keys[0], (PROMPT_TOTAL,), TAIL_TOKENS // 2, TAIL_TOKENS + 1)
    longest = jax.random.randint(split_random_keys[1], (), 0, PROMPT_TOTAL)
    return jnp.where(jnp.arange(PROMPT_TOTAL) == longest, TAIL_TOKENS, drawn).astype(jnp.int32)


def steps_of(stream_key, extent, cuts, low, largest):
    loudness, own = 1.0, jax.random.fold_in(stream_key, 6)
    for position, parts in cuts:
        heights = jnp.exp(jax.random.uniform(jax.random.fold_in(own, position), (parts,), jnp.float32, low / len(cuts), largest / len(cuts)))
        loudness = loudness * jnp.repeat(heights, extent[position] // parts).reshape([-1 if axis == position else 1 for axis in range(len(extent))])
    return loudness


def centred(stream_key, dims, scale, reach, cuts=(), held_as=jnp.bfloat16):
    values = scale * jax.random.normal(stream_key, dims, jnp.float32)
    if cuts:
        values = values * steps_of(stream_key, dims, cuts, -0.22, 0.18)
    return jnp.clip(values, -reach, reach).astype(held_as)


def setup_inputs(seed: int = 0, part: int = 0) -> dict:
    key_of = jax.random.split(jax.random.key(seed), 17)
    own_keys = jax.random.split(jax.random.fold_in(key_of[16], part), 17)
    x_pre = draw_x_pre(jax.random.fold_in(jax.random.fold_in(key_of[16], part), 71), part)
    z_pre = centred(own_keys[1], (PROMPT_TOTAL, TAIL_TOKENS, INNER), 1.0, 6.0, ((0, 4), (2, 4)))
    b_pre = centred(own_keys[2], (PROMPT_TOTAL, TAIL_TOKENS, G * N), 0.3, 1.796875, ((0, 4),))
    c_pre = centred(own_keys[3], (PROMPT_TOTAL, TAIL_TOKENS, G * N), 0.09, 0.5390625, ((0, 4),))
    dt_pre = draw_dt_pre(jax.random.fold_in(jax.random.fold_in(key_of[16], part), 71), part)
    lengths = draw_lengths(jax.random.fold_in(jax.random.fold_in(key_of[16], part), 71), part)
    init_state = centred(own_keys[6], (PROMPT_TOTAL, N, INNER), 1.0, 6.0, ((0, 4), (2, 4)), jnp.float32)
    a_rates = draw_a_rates(jax.random.fold_in(key_of[16], 71), part)
    dt_bias = jnp.clip(-2.0 + 1.0 * jax.random.uniform(key_of[8], (H,), jnp.float32) ** steps_of(key_of[8], (H,), ((0, 4),), -0.2, 0.2), -2.0, -1.0)
    skip_scale = jnp.clip(0.5 + 1.5 * jax.random.uniform(key_of[9], (H,), jnp.float32) ** steps_of(key_of[9], (H,), ((0, 4),), -0.2, 0.2), 0.5, 2.0)
    norm_gain = jnp.clip(1.0 + 0.1 * jax.random.normal(key_of[10], (INNER,), jnp.float32), 0.5, 1.5)
    x_dec = draw_x_dec(jax.random.fold_in(jax.random.fold_in(key_of[16], part), 71), part)
    z_dec = centred(own_keys[12], (SLOTS, PROMPT_TOTAL, INNER), 1.0, 6.0, ((0, 4), (2, 4)))
    b_dec = centred(own_keys[13], (SLOTS, PROMPT_TOTAL, G * N), 1.0, 6.0, ((0, 4),))
    c_dec = centred(own_keys[14], (SLOTS, PROMPT_TOTAL, G * N), 0.09, 0.5390625, ((0, 4),))
    dt_dec = centred(own_keys[15], (SLOTS, PROMPT_TOTAL, H), 0.5, 3.0, ((0, 4), (2, 4)), jnp.float32)
    return {"x_pre": x_pre, "z_pre": z_pre, "b_pre": b_pre, "c_pre": c_pre, "dt_pre": dt_pre, "lengths": lengths, "init_state": init_state, "a_rates": a_rates, "dt_bias": dt_bias, "skip_scale": skip_scale, "norm_gain": norm_gain, "x_dec": x_dec, "z_dec": z_dec, "b_dec": b_dec, "c_dec": c_dec, "dt_dec": dt_dec}


epsilon = 1e-05
highest = lax.Precision.HIGHEST

def group_pick(first_head, head_count):
    head_ids = first_head + jnp.arange(head_count, dtype=jnp.int32)
    owners = head_ids // (H // G)
    return (owners[:, None] == jnp.arange(G, dtype=jnp.int32)[None, :]).astype(jnp.float32)

def scan_prompt(inputs, b_rows, c_rows, step_delta, rates, skip_gain, start_state, picker):
    length = inputs.shape[0]
    head_count = step_delta.shape[1]
    head_width = inputs.shape[1] // head_count
    states = b_rows.shape[1] // G
    blocks = length // BLOCK
    b_head = jnp.einsum('tgn,hg->thn', b_rows.astype(jnp.float32).reshape(length, G, states), picker, precision=highest)
    c_head = jnp.einsum('tgn,hg->thn', c_rows.astype(jnp.float32).reshape(length, G, states), picker, precision=highest)
    b_head = b_head.reshape(blocks, BLOCK, head_count, states)
    c_head = c_head.reshape(blocks, BLOCK, head_count, states)
    values = inputs.astype(jnp.float32).reshape(blocks, BLOCK, head_count, head_width)
    block_delta = step_delta.reshape(blocks, BLOCK, head_count)
    decays = jnp.cumsum(-block_delta * rates, axis=1)
    causal_mask = (jnp.arange(BLOCK)[:, None] >= jnp.arange(BLOCK)[None, :])[None, :, :, None]
    spread = decays[:, :, None, :] - decays[:, None, :, :]
    weights = jnp.where(causal_mask, jnp.exp(jnp.where(causal_mask, spread, 0.0)), 0.0)
    scores = jnp.einsum('cihn,cjhn->cijh', c_head, b_head, precision=highest) * weights * block_delta[:, None, :, :]
    inner_part = jnp.einsum('cijh,cjhp->cihp', scores, values, precision=highest)
    tail_decay = jnp.exp(decays[:, -1:, :] - decays) * block_delta
    block_states = jnp.einsum('cjhn,cjhp->cnhp', b_head * tail_decay[..., None], values, precision=highest)
    block_totals = jnp.exp(decays[:, -1, :])

    def carry_step(carried, pieces):
        factor, fresh_term = pieces
        return (factor[None, :, None] * carried + fresh_term, carried)
    final_carry, starts = lax.scan(carry_step, start_state.reshape(states, head_count, head_width), (block_totals, block_states))
    outer_part = jnp.einsum('cihn,cnhp->cihp', c_head, starts, precision=highest) * jnp.exp(decays)[..., None]
    result = inner_part + outer_part + skip_gain[None, None, :, None] * values
    return (result.reshape(length, head_count * head_width), final_carry.reshape(states, head_count * head_width))

def gate_values(result, gate_rows):
    gate_rows = gate_rows.astype(jnp.float32)
    return result * gate_rows * jax.nn.sigmoid(gate_rows)

def reference(x_pre, z_pre, b_pre, c_pre, dt_pre, lengths, init_state, a_rates, dt_bias, skip_scale, norm_gain, x_dec, z_dec, b_dec, c_dec, dt_dec):
    positions = jnp.arange(TAIL_TOKENS, dtype=jnp.int32)
    valid_mask = (positions[None, :] < lengths[:, None]).astype(jnp.float32)
    step_delta = jax.nn.softplus(dt_pre + dt_bias) * valid_mask[:, :, None]
    picker = group_pick(0, H)

    def one_prompt(pieces):
        inputs, b_rows, c_rows, prompt_delta, start_state = pieces
        return scan_prompt(inputs, b_rows, c_rows, prompt_delta, a_rates, skip_scale, start_state, picker)
    result, final_carry = lax.map(one_prompt, (x_pre, b_pre, c_pre, step_delta, init_state))
    final_state = final_carry.astype(jnp.bfloat16)
    gated_rows = gate_values(result, z_pre)
    norm_scale = lax.rsqrt(lax.optimization_barrier(jnp.mean(gated_rows * gated_rows, axis=-1, keepdims=True)) + epsilon)
    out_pre = (gated_rows * norm_scale * norm_gain * valid_mask[:, :, None]).astype(jnp.bfloat16)
    slot_count = x_dec.shape[0]
    prompt_count = x_dec.shape[1]
    c_groups = c_dec.astype(jnp.float32).reshape(slot_count, prompt_count, G, N)
    b_groups = b_dec.astype(jnp.float32).reshape(slot_count, prompt_count, G, N)
    c_head = jnp.einsum('spgn,hg->sphn', c_groups, picker, precision=highest)
    cached = final_state.astype(jnp.float32).reshape(prompt_count, N, H, P_SIZE)
    state_reads = jnp.einsum('sphn,pnhq->sphq', c_head, cached, precision=highest)
    cb_dot = jnp.einsum('spgn,spgn->spg', c_groups, b_groups, precision=highest)
    cb_dot = jnp.einsum('spg,hg->sph', cb_dot, picker, precision=highest)
    step_sizes = jax.nn.softplus(dt_dec + dt_bias)
    decay_rate = jnp.exp(-step_sizes * a_rates)
    values = x_dec.astype(jnp.float32).reshape(slot_count, prompt_count, H, P_SIZE)
    fresh_term = decay_rate[..., None] * state_reads + (step_sizes * cb_dot + skip_scale)[..., None] * values
    gated_dec = gate_values(fresh_term.reshape(slot_count, prompt_count, H * P_SIZE), z_dec)
    dec_scale = lax.rsqrt(lax.optimization_barrier(jnp.mean(gated_dec * gated_dec, axis=-1, keepdims=True)) + epsilon)
    out_dec = (gated_dec * dec_scale * norm_gain).astype(jnp.bfloat16)
    return (out_pre, final_state, out_dec)
```

```python
import functools

import jax
import jax.numpy as jnp
from jax import lax
from jax.experimental import pallas as pl
from jax.experimental.pallas import tpu as pltpu
from jax.sharding import PartitionSpec as P

H = 128
G = 4
epsilon = 1e-05
highest = lax.Precision.HIGHEST
f32 = jnp.float32
bf16 = jnp.bfloat16
LOG2E = 1.4426950408889634
CAP = 100.0


def softplus(v):
    return jnp.maximum(v, 0.0) + jnp.log1p(jnp.exp(-jnp.abs(v)))


def silu(z):
    half = 0.5 * z
    return half * (1.0 + jnp.tanh(half))


def split(v, parts):
    out = []
    for _ in range(parts):
        piece = v.astype(bf16)
        out.append(piece)
        v = v - piece.astype(f32)
    return out


def widen(v, width, parts):
    heads = v.shape[1]
    per = width // heads
    row = lax.broadcasted_iota(jnp.int32, (heads, width), 0)
    lane = lax.broadcasted_iota(jnp.int32, (heads, width), 1)
    pick = jnp.where((lane >= row * per) & (lane < (row + 1) * per), 1.0, 0.0).astype(bf16)
    lhs = jnp.concatenate(split(v, parts), axis=1)
    rhs = jnp.concatenate([pick] * parts, axis=0)
    return jnp.dot(lhs, rhs, preferred_element_type=f32)


def group_lanes(states, heads_here):
    start = (lax.axis_index("head") * heads_here) // (H // G)
    return pl.ds(pl.multiple_of(start * states, states), states)


def state_kernel(len_ref, x_ref, b_ref, dt_ref, s0_ref, a_ref, bias_ref, fs_ref, c_ref, r_ref):
    length, heads = dt_ref.shape
    width = x_ref.shape[1]
    states = s0_ref.shape[0]
    valid = lax.broadcasted_iota(jnp.int32, (length, heads), 0) < len_ref[0]
    delta = jnp.where(valid, softplus(dt_ref[...] + bias_ref[...]), 0.0)
    rate = delta * a_ref[...] * (-LOG2E)
    row = lax.broadcasted_iota(jnp.int32, (length, length), 0)
    lane = lax.broadcasted_iota(jnp.int32, (length, length), 1)
    lower = jnp.where(row >= lane, 1.0, 0.0).astype(bf16)
    sums = jnp.dot(
        jnp.concatenate([lower] * 3, axis=1),
        jnp.concatenate(split(rate, 3), axis=0),
        preferred_element_type=f32,
    )
    c_ref[...] = sums
    r_ref[...] = jnp.log2(delta) - sums
    last = sums[length - 1 :, :]
    weight = jnp.exp2(last - sums) * delta
    total = widen(jnp.exp2(last), width, 2)
    wide = widen(weight, width, 2)
    xw = (x_ref[...].astype(f32) * wide).astype(bf16)
    b = b_ref[:, group_lanes(states, heads)]
    fresh = lax.dot_general(b, xw, (((0,), (0,)), ((), ())), preferred_element_type=f32)
    fs_ref[...] = (fresh + total * s0_ref[...]).astype(bf16)


def read_kernel(*refs):
    n = (len(refs) - 1) // 2
    fs_ref = refs[0]
    states, width = fs_ref.shape
    heads = width // 64
    me = lax.axis_index("sample")
    lanes = group_lanes(states, heads)
    rows = []
    for k in range(n):
        block = refs[1 + k][:, lanes].astype(f32)
        mine = lax.broadcasted_iota(jnp.int32, block.shape, 0) == me
        rows.append(jnp.sum(jnp.where(mine, block, 0.0), axis=0, keepdims=True))
    q = jnp.concatenate(rows, axis=0).astype(bf16)
    reads = jnp.dot(q, fs_ref[...], preferred_element_type=f32)
    for k in range(n):
        refs[1 + n + k][...] = reads[k : k + 1, :]


def prompt_kernel(
    x_ref, z_ref, b_ref, cp_ref, s0_ref, c_ref, r_ref, skip_ref, gated_ref, sq_ref, m_ref
):
    length, heads = c_ref.shape
    states, width = s0_ref.shape
    per = width // heads
    lanes = group_lanes(states, heads)
    cp = cp_ref[:, lanes]
    scores = lax.dot_general(
        cp, b_ref[:, lanes], (((1,), (1,)), ((), ())), preferred_element_type=f32
    )
    row = lax.broadcasted_iota(jnp.int32, (length, length), 0)
    lane = lax.broadcasted_iota(jnp.int32, (length, length), 1)
    scores = jnp.where(row >= lane, scores, 0.0)
    m_ref[...] = jnp.dot(cp, s0_ref[...].astype(bf16), preferred_element_type=f32)
    skip = widen(skip_ref[...], width, 3)
    rt = r_ref[...].T
    c = c_ref[...]
    pair = 2 * per
    low = lax.broadcasted_iota(jnp.int32, (length, pair), 1) < per
    squares = jnp.zeros((length, pair), f32)
    for q in range(heads // 2):
        ch = slice(q * pair, (q + 1) * pair)
        x = x_ref[:, ch]
        xf = x.astype(f32)
        x_cat = jnp.concatenate(
            [jnp.where(low, xf, 0.0).astype(bf16), jnp.where(low, 0.0, xf).astype(bf16)], axis=0
        )
        parts = []
        cols = []
        for h in (2 * q, 2 * q + 1):
            col = jnp.broadcast_to(c[:, h : h + 1], (length, length))
            arg = jnp.minimum(col + rt[h : h + 1, :], CAP)
            parts.append((jnp.exp2(arg) * scores).astype(bf16))
            cols.append(col)
        y = jnp.dot(jnp.concatenate(parts, axis=1), x_cat, preferred_element_type=f32)
        decay = jnp.exp2(jnp.where(low, cols[0], cols[1]))
        y = y + decay * m_ref[:, ch] + skip[:, ch] * xf
        gated = y * silu(z_ref[:, ch].astype(f32))
        gated_ref[:, ch] = gated
        squares = squares + gated * gated
    total = jnp.broadcast_to(jnp.sum(squares, axis=1, keepdims=True), (length, length))
    sq_ref[...] = total.T[0:1, :]


def slot_kernel(*refs, states):
    (sq_ref, x_ref, z_ref, b_ref, c_ref, dt_ref, a_ref, bias_ref, skip_ref) = refs[:9]
    read_refs = refs[9:-2]
    gated_ref, pay_ref = refs[-2:]
    prompts, width = x_ref.shape
    heads = dt_ref.shape[1]
    me = lax.axis_index("sample")
    lanes = group_lanes(states, heads)
    step = softplus(dt_ref[...] + bias_ref[...])
    decay = jnp.exp(-step * a_ref[...])
    cb = jnp.sum(c_ref[:, lanes].astype(f32) * b_ref[:, lanes].astype(f32), axis=1, keepdims=True)
    gain = step * cb + skip_ref[...]
    wide = widen(jnp.concatenate([decay, gain], axis=0), width, 3)
    prompt = lax.broadcasted_iota(jnp.int32, (prompts, width), 0)
    reads = jnp.zeros((prompts, width), f32)
    for k, ref in enumerate(read_refs):
        reads = jnp.where(prompt == (me ^ k), ref[...], reads)
    mix = wide[:prompts] * reads + wide[prompts:] * x_ref[...].astype(f32)
    gated = mix * silu(z_ref[...].astype(f32))
    gated_ref[...] = gated
    total = jnp.broadcast_to(jnp.sum(gated * gated, axis=1, keepdims=True), (prompts, 128))
    row = lax.broadcasted_iota(jnp.int32, (prompts, 128), 0)
    lane = lax.broadcasted_iota(jnp.int32, (prompts, 128), 1)
    pay_ref[0:1, :] = sq_ref[...]
    pay_ref[1:2, :] = jnp.sum(jnp.where(row == lane, total, 0.0), axis=0, keepdims=True)


def norm_kernel(*refs, channels):
    len_ref, gated_ref, dec_ref, gain_ref = refs[:4]
    pay_refs = refs[4:-2]
    out_ref, out_dec_ref = refs[-2:]
    length = gated_ref.shape[0]
    prompts = dec_ref.shape[0]
    total = pay_refs[0][...]
    for ref in pay_refs[1:]:
        total = total + ref[...]
    scale = lax.rsqrt(total * (1.0 / channels) + epsilon)
    column = jnp.broadcast_to(scale[0:1, :], (length, length)).T[:, 0:1]
    valid = lax.broadcasted_iota(jnp.int32, (length, 1), 0) < len_ref[0]
    column = jnp.where(valid, column, 0.0)
    gain = gain_ref[...]
    out_ref[...] = (gated_ref[...] * column * gain).astype(bf16)
    row = lax.broadcasted_iota(jnp.int32, (prompts, 128), 0)
    lane = lax.broadcasted_iota(jnp.int32, (prompts, 128), 1)
    wide = jnp.broadcast_to(scale[1:2, :], (prompts, 128))
    dec = jnp.sum(jnp.where(row == lane, wide, 0.0), axis=1, keepdims=True)
    out_dec_ref[...] = (dec_ref[...] * dec * gain).astype(bf16)


smem = pl.BlockSpec(memory_space=pltpu.SMEM)
vmem = pl.BlockSpec(memory_space=pltpu.VMEM)


def call(kernel, name, ins, outs, smem_ins=0, scratch=()):
    return pl.pallas_call(
        kernel,
        name=name,
        in_specs=[smem] * smem_ins + [vmem] * (len(ins) - smem_ins),
        out_specs=tuple(vmem for _ in outs),
        out_shape=tuple(jax.ShapeDtypeStruct(s, d) for s, d in outs),
        scratch_shapes=list(scratch),
    )(*ins)


def make_body(mesh):
    samples = mesh.shape["sample"]
    head_parts = mesh.shape["head"]

    def swap(v, axis, k):
        return lax.ppermute(v, axis, [(i, i ^ k) for i in range(mesh.shape[axis])])

    def body(
        x_pre, z_pre, b_pre, c_pre, dt_pre, lengths, init_state, a_rates, dt_bias, skip_scale,
        norm_gain, x_dec, z_dec, b_dec, c_dec, dt_dec,
    ):
        length, width = x_pre.shape[1:]
        states = init_state.shape[1]
        heads = a_rates.shape[0]
        prompts = x_dec.shape[1]
        x, z, b, cp, dt, s0 = (v[0] for v in (x_pre, z_pre, b_pre, c_pre, dt_pre, init_state))
        xd, zd, bd, cd, dtd = (v[0] for v in (x_dec, z_dec, b_dec, c_dec, dt_dec))
        a, bias, skip = (v[None] for v in (a_rates, dt_bias, skip_scale))
        queries = [cd] + [swap(cd, "sample", k) for k in range(1, samples)]
        fs, c, r = call(
            state_kernel, "state", (lengths, x, b, dt, s0, a, bias),
            (((states, width), bf16), ((length, heads), f32), ((length, heads), f32)), 1,
        )
        reads = call(read_kernel, "read", (fs, *queries), (((1, width), f32),) * samples)
        reads = [reads[0]] + [swap(reads[k], "sample", k) for k in range(1, samples)]
        gated, sq = call(
            prompt_kernel, "prompt", (x, z, b, cp, s0, c, r, skip),
            (((length, width), f32), ((1, length), f32)), 0,
            (pltpu.VMEM((length, width), f32),),
        )
        gated_dec, pay = call(
            functools.partial(slot_kernel, states=states), "slot",
            (sq, xd, zd, bd, cd, dtd, a, bias, skip, *reads),
            (((prompts, width), f32), ((2, 128), f32)),
        )
        pays = [pay] + [swap(pay, "head", k) for k in range(1, head_parts)]
        out_pre, out_dec = call(
            functools.partial(norm_kernel, channels=width * head_parts), "norm",
            (lengths, gated, gated_dec, norm_gain[None], *pays),
            (((length, width), bf16), ((prompts, width), bf16)), 1,
        )
        return out_pre[None], fs[None], out_dec[None]

    return body


def solution(mesh):
    tokens = P(("rep", "sample"), None, "head")
    groups = P(("rep", "sample"), None, None)
    in_specs = (
        tokens, tokens, groups, groups, tokens, P(("rep", "sample")), tokens,
        P("head"), P("head"), P("head"), P("head"), tokens, tokens, groups, groups, tokens,
    )
    return jax.shard_map(
        make_body(mesh), mesh=mesh, in_specs=in_specs, out_specs=(tokens,) * 3, check_vma=False
    )
```

```python
import functools

import jax
import jax.numpy as jnp
from jax import lax
from jax.experimental import pallas as pl
from jax.experimental.pallas import tpu as pltpu
from jax.sharding import PartitionSpec as P

H = 128
G = 4
epsilon = 1e-05
highest = lax.Precision.HIGHEST
f32 = jnp.float32
bf16 = jnp.bfloat16
LOG2E = 1.4426950408889634
CAP = 100.0
CHUNKS = 4
GRANT = 16 << 20


def softplus(v):
    return jnp.maximum(v, 0.0) + jnp.log1p(jnp.exp(-jnp.abs(v)))


def silu(z):
    half = 0.5 * z
    return half * (1.0 + jnp.tanh(half))


def split(v, parts):
    out = []
    for _ in range(parts):
        piece = v.astype(bf16)
        out.append(piece)
        v = v - piece.astype(f32)
    return out


def widen(v, width, parts):
    heads = v.shape[1]
    per = width // heads
    row = lax.broadcasted_iota(jnp.int32, (heads, width), 0)
    lane = lax.broadcasted_iota(jnp.int32, (heads, width), 1)
    pick = jnp.where((lane >= row * per) & (lane < (row + 1) * per), 1.0, 0.0).astype(bf16)
    lhs = jnp.concatenate(split(v, parts), axis=1)
    rhs = jnp.concatenate([pick] * parts, axis=0)
    return jnp.dot(lhs, rhs, preferred_element_type=f32)


def group_lanes(states, heads_here):
    start = (lax.axis_index("head") * heads_here) // (H // G)
    return pl.ds(pl.multiple_of(start * states, states), states)


def as_column(row):
    n = row.shape[1]
    wide = jnp.broadcast_to(row, (n, n))
    here = lax.broadcasted_iota(jnp.int32, (n, n), 0) == lax.broadcasted_iota(jnp.int32, (n, n), 1)
    return jnp.sum(jnp.where(here, wide, 0.0), axis=1, keepdims=True)


def widen_columns(v, width, parts):
    heads = v.shape[0]
    per = width // heads
    row = lax.broadcasted_iota(jnp.int32, (heads, width), 0)
    lane = lax.broadcasted_iota(jnp.int32, (heads, width), 1)
    pick = jnp.where((lane >= row * per) & (lane < (row + 1) * per), 1.0, 0.0).astype(bf16)
    lhs = jnp.concatenate(split(v, parts), axis=0)
    rhs = jnp.concatenate([pick] * parts, axis=0)
    return lax.dot_general(lhs, rhs, (((0,), (0,)), ((), ())), preferred_element_type=f32)


def state_kernel(
    len_hbm, dt_hbm, a_hbm, bias_hbm, x_hbm, b_hbm, s0_hbm, z_hbm, cp_hbm,
    fs_ref, c_ref, r_ref, valid_ref, x_ref, b_ref, s0_ref, z_ref, cp_ref,
    len_ref, dt_ref, a_ref, bias_ref, sems,
):
    heads, length = dt_ref.shape
    width = x_ref.shape[1]
    states = s0_ref.shape[0]
    lanes = group_lanes(states, heads)
    copies = [
        pltpu.make_async_copy(source, target, sems.at[i])
        for i, (source, target) in enumerate((
            (len_hbm, len_ref), (dt_hbm, dt_ref), (a_hbm, a_ref), (bias_hbm, bias_ref),
            (x_hbm, x_ref), (b_hbm.at[:, lanes], b_ref), (s0_hbm, s0_ref),
            (z_hbm, z_ref), (cp_hbm.at[:, lanes], cp_ref),
        ))
    ]
    for copy in copies:
        copy.start()
    row = lax.broadcasted_iota(jnp.int32, (length, length), 0)
    lane = lax.broadcasted_iota(jnp.int32, (length, length), 1)
    upper = jnp.where(row <= lane, 1.0, 0.0).astype(bf16)
    for copy in copies[:4]:
        copy.wait()
    valid = lax.broadcasted_iota(jnp.int32, (heads, length), 1) < len_ref[0]
    delta = jnp.where(valid, softplus(dt_ref[...] + as_column(bias_ref[...])), 0.0)
    rate = delta * as_column(a_ref[...]) * (-LOG2E)
    sums = jnp.dot(
        jnp.concatenate(split(rate, 3), axis=1),
        jnp.concatenate([upper] * 3, axis=0),
        preferred_element_type=f32,
    )
    rows = lax.broadcasted_iota(jnp.int32, valid_ref.shape, 0)
    valid_ref[...] = jnp.where(rows < len_ref[0], 1.0, 0.0)
    c_ref[...] = sums.T
    r_ref[...] = jnp.log2(delta) - sums
    last = sums[:, length - 1 :]
    weight = jnp.exp2(last - sums) * delta
    total = widen_columns(jnp.broadcast_to(jnp.exp2(last), (heads, 8)), width, 2)[0:1, :]
    wide = widen_columns(weight, width, 2)
    copies[4].wait()
    copies[5].wait()
    xw = (x_ref[...].astype(f32) * wide).astype(bf16)
    fresh = lax.dot_general(b_ref[...], xw, (((0,), (0,)), ((), ())), preferred_element_type=f32)
    copies[6].wait()
    fs_ref[...] = (fresh + total * s0_ref[...]).astype(bf16)
    copies[7].wait()
    copies[8].wait()


def read_kernel(*refs):
    n = (len(refs) - 1) // 2
    fs_ref = refs[0]
    states, width = fs_ref.shape
    heads = width // 64
    me = lax.axis_index("sample")
    lanes = group_lanes(states, heads)
    rows = []
    for k in range(n):
        block = refs[1 + k][:, lanes].astype(f32)
        mine = lax.broadcasted_iota(jnp.int32, block.shape, 0) == me
        rows.append(jnp.sum(jnp.where(mine, block, 0.0), axis=0, keepdims=True))
    q = jnp.concatenate(rows, axis=0).astype(bf16)
    reads = jnp.dot(q, fs_ref[...], preferred_element_type=f32)
    for k in range(n):
        refs[1 + n + k][...] = reads[k : k + 1, :]


def prompt_kernel(
    fs_ref, x_ref, z_ref, b_ref, cp_ref, s0_ref, c_ref, r_ref, skip_ref, gain_ref,
    xd_ref, zd_ref, bd_ref, cd_ref, dtd_ref, a_ref, bias_ref,
    gated_ref, sq_ref, u_ref, v_ref, fs_hbm, m_ref, sem,
):
    length, heads = c_ref.shape
    states, width = s0_ref.shape
    per = width // heads
    prompts = xd_ref.shape[0]
    lanes = group_lanes(states, heads)
    store = pltpu.make_async_copy(fs_ref, fs_hbm, sem)
    store.start()
    cp = cp_ref[...]
    scores = lax.dot_general(cp, b_ref[...], (((1,), (1,)), ((), ())), preferred_element_type=f32)
    row = lax.broadcasted_iota(jnp.int32, (length, length), 0)
    lane = lax.broadcasted_iota(jnp.int32, (length, length), 1)
    scores = jnp.where(row >= lane, scores, 0.0)
    m_ref[...] = jnp.dot(cp, s0_ref[...].astype(bf16), preferred_element_type=f32)

    step = softplus(dtd_ref[...] + bias_ref[...])
    cb = cd_ref[:, lanes].astype(f32) * bd_ref[:, lanes].astype(f32)
    cb = jnp.sum(cb, axis=1, keepdims=True)
    gain = step * cb + skip_ref[...]
    skips = jnp.broadcast_to(skip_ref[...], (8, heads))
    wide = widen(jnp.concatenate([jnp.exp(-step * a_ref[...]), gain], axis=0), width, 3)
    skip = widen(skips, width, 3)[0:1, :]
    gate = silu(zd_ref[...].astype(f32))
    u_ref[...] = wide[:prompts] * gate
    v_ref[...] = wide[prompts:] * xd_ref[...].astype(f32) * gate

    rt = r_ref[...]
    c = c_ref[...]
    pair = 2 * per
    low = lax.broadcasted_iota(jnp.int32, (length, pair), 1) < per
    squares = jnp.zeros((length, pair), f32)
    for q in range(heads // 2):
        ch = slice(q * pair, (q + 1) * pair)
        x = x_ref[:, ch]
        xf = x.astype(f32)
        x_cat = jnp.concatenate(
            [jnp.where(low, xf, 0.0).astype(bf16), jnp.where(low, 0.0, xf).astype(bf16)], axis=0
        )
        parts = []
        cols = []
        for h in (2 * q, 2 * q + 1):
            col = jnp.broadcast_to(c[:, h : h + 1], (length, length))
            arg = jnp.minimum(col + rt[h : h + 1, :], CAP)
            parts.append((jnp.exp2(arg) * scores).astype(bf16))
            cols.append(col)
        y = jnp.dot(jnp.concatenate(parts, axis=1), x_cat, preferred_element_type=f32)
        decay = jnp.exp2(jnp.where(low, cols[0], cols[1]))
        y = y + decay * m_ref[:, ch] + skip[:, ch] * xf
        gated = y * silu(z_ref[:, ch].astype(f32))
        gated_ref[:, ch] = gated * gain_ref[:, ch]
        squares = squares + gated * gated
    total = jnp.broadcast_to(jnp.sum(squares, axis=1, keepdims=True), (length, length))
    sq_ref[...] = total.T[0:1, :]
    store.wait()


def slot_kernel(*refs):
    sq_ref, u_ref, v_ref = refs[:3]
    read_refs = refs[3:-2]
    gated_ref, pay_ref = refs[-2:]
    prompts, width = u_ref.shape
    me = lax.axis_index("sample")
    prompt = lax.broadcasted_iota(jnp.int32, (prompts, width), 0)
    reads = jnp.zeros((prompts, width), f32)
    for k, ref in enumerate(read_refs):
        reads = jnp.where(prompt == (me ^ k), ref[...], reads)
    gated = u_ref[...] * reads + v_ref[...]
    gated_ref[...] = gated
    total = jnp.broadcast_to(jnp.sum(gated * gated, axis=1, keepdims=True), (prompts, 128))
    row = lax.broadcasted_iota(jnp.int32, (prompts, 128), 0)
    lane = lax.broadcasted_iota(jnp.int32, (prompts, 128), 1)
    pay_ref[0:1, :] = sq_ref[...]
    pay_ref[1:2, :] = jnp.sum(jnp.where(row == lane, total, 0.0), axis=0, keepdims=True)


def norm_kernel(*refs, channels, payloads):
    valid_ref, gated_ref, dec_ref, gain_ref = refs[:4]
    pay_refs = refs[4 : 4 + payloads]
    out_hbm, dec_hbm, out_ref, out_dec_ref, sems = refs[4 + payloads :]
    length = gated_ref.shape[0]
    prompts = dec_ref.shape[0]
    total = pay_refs[0][...]
    for ref in pay_refs[1:]:
        total = total + ref[...]
    scale = lax.rsqrt(total * (1.0 / channels) + epsilon)
    row = lax.broadcasted_iota(jnp.int32, (prompts, 128), 0)
    lane = lax.broadcasted_iota(jnp.int32, (prompts, 128), 1)
    wide = jnp.broadcast_to(scale[1:2, :], (prompts, 128))
    dec = jnp.sum(jnp.where(row == lane, wide, 0.0), axis=1, keepdims=True)
    out_dec_ref[...] = (dec_ref[...] * dec * gain_ref[...]).astype(bf16)
    copies = [pltpu.make_async_copy(out_dec_ref, dec_hbm, sems.at[0])]
    copies[0].start()
    column = jnp.broadcast_to(scale[0:1, :], (length, length)).T * valid_ref[...]
    column = column[:, 0:1]
    for i in range(CHUNKS):
        rows = slice(i * length // CHUNKS, (i + 1) * length // CHUNKS)
        out_ref[rows, :] = (gated_ref[rows, :] * column[rows, :]).astype(bf16)
        copies.append(
            pltpu.make_async_copy(out_ref.at[rows, :], out_hbm.at[rows, :], sems.at[1 + i])
        )
        copies[-1].start()
    for copy in copies:
        copy.wait()


VMEM = pltpu.MemorySpace.VMEM
HBM = pltpu.MemorySpace.HBM


def call(kernel, name, ins, outs, scratch=(), far=(), fetch=False):
    space = HBM if fetch else VMEM
    outs = [(VMEM, *out) for out in outs] + [(HBM, *out) for out in far]
    return pl.pallas_call(
        kernel,
        name=name,
        in_specs=[pl.BlockSpec(memory_space=pl.ANY if v.size == 1 else space) for v in ins],
        out_specs=tuple(pl.BlockSpec(memory_space=out[0]) for out in outs),
        out_shape=tuple(out[0](*out[1:]) for out in outs),
        scratch_shapes=list(scratch),
        compiler_params=pltpu.CompilerParams(vmem_limit_bytes=GRANT),
    )(*(v if v.size == 1 else pltpu.with_memory_space_constraint(v, space) for v in ins))


def make_body(mesh):
    samples = mesh.shape["sample"]
    head_parts = mesh.shape["head"]

    def swap(v, axis, k):
        return lax.ppermute(v, axis, [(i, i ^ k) for i in range(mesh.shape[axis])])

    def body(
        x_pre, z_pre, b_pre, c_pre, dt_pre, lengths, init_state, a_rates, dt_bias, skip_scale,
        norm_gain, x_dec, z_dec, b_dec, c_dec, dt_dec,
    ):
        length, width = x_pre.shape[1:]
        states = init_state.shape[1]
        heads = a_rates.shape[0]
        prompts = x_dec.shape[1]
        x, z, b, cp, dt, s0 = (v[0] for v in (x_pre, z_pre, b_pre, c_pre, dt_pre, init_state))
        xd, zd, bd, cd, dtd = (v[0] for v in (x_dec, z_dec, b_dec, c_dec, dt_dec))
        a, bias, skip, gain = (v[None] for v in (a_rates, dt_bias, skip_scale, norm_gain))
        queries = [cd] + [swap(cd, "sample", k) for k in range(1, samples)]
        fs, c, r, valid, x, b, s0, z, cp = call(
            state_kernel, "state", (lengths, dt.T, a, bias, x, b, s0, z, cp),
            (
                ((states, width), bf16), ((length, heads), f32), ((heads, length), f32),
                ((length, 128), f32), ((length, width), bf16), ((length, states), bf16), ((states, width), f32),
                ((length, width), bf16), ((length, states), bf16),
            ),
            (
                pltpu.SMEM((1,), jnp.int32), pltpu.VMEM((heads, length), f32),
                pltpu.VMEM((1, heads), f32), pltpu.VMEM((1, heads), f32),
                pltpu.SemaphoreType.DMA((9,)),
            ), fetch=True,
        )
        reads = call(read_kernel, "read", (fs, *queries), (((1, width), f32),) * samples)
        reads = [reads[0]] + [swap(reads[k], "sample", k) for k in range(1, samples)]
        gated, sq, u, v, fs = call(
            prompt_kernel, "prompt",
            (fs, x, z, b, cp, s0, c, r, skip, gain, xd, zd, bd, cd, dtd, a, bias),
            (((length, width), f32), ((1, length), f32)) + (((prompts, width), f32),) * 2,
            (pltpu.VMEM((length, width), f32), pltpu.SemaphoreType.DMA(())),
            (((states, width), bf16),),
        )
        gated_dec, pay = call(
            slot_kernel, "slot", (sq, u, v, *reads), (((prompts, width), f32), ((2, 128), f32))
        )
        pays = [pay] + [swap(pay, "head", k) for k in range(1, head_parts)]
        out_pre, out_dec = call(
            functools.partial(norm_kernel, channels=width * head_parts, payloads=head_parts),
            "norm", (valid, gated, gated_dec, gain, *pays), (),
            (
                pltpu.VMEM((length, width), bf16), pltpu.VMEM((prompts, width), bf16),
                pltpu.SemaphoreType.DMA((1 + CHUNKS,)),
            ), (((length, width), bf16), ((prompts, width), bf16)),
        )
        return out_pre[None], fs[None], out_dec[None]

    return body


def solution(mesh):
    tokens = P(("rep", "sample"), None, "head")
    groups = P(("rep", "sample"), None, None)
    in_specs = (
        tokens, tokens, groups, groups, tokens, P(("rep", "sample")), tokens,
        P("head"), P("head"), P("head"), P("head"), tokens, tokens, groups, groups, tokens,
    )
    return jax.shard_map(
        make_body(mesh), mesh=mesh, in_specs=in_specs, out_specs=(tokens,) * 3, check_vma=False
    )
```

```python
import functools

import jax
import jax.numpy as jnp
from jax import lax
from jax.experimental import pallas as pl
from jax.experimental.pallas import tpu as pltpu
from jax.sharding import PartitionSpec as P


H = 128
G = 4
epsilon = 1e-05
f32 = jnp.float32
bf16 = jnp.bfloat16
LOG2E = 1.4426950408889634
CAP = 100.0
CHUNKS = 4
GRANT = 16 << 20


def softplus(v):
    return jnp.maximum(v, 0.0) + jnp.log1p(jnp.exp(-jnp.abs(v)))


def silu(z):
    half = 0.5 * z
    return half * (1.0 + jnp.tanh(half))


def split(v, parts):
    out = []
    for _ in range(parts):
        piece = v.astype(bf16)
        out.append(piece)
        v = v - piece.astype(f32)
    return out


def widen(v, width, parts):
    heads = v.shape[1]
    per = width // heads
    row = lax.broadcasted_iota(jnp.int32, (heads, width), 0)
    lane = lax.broadcasted_iota(jnp.int32, (heads, width), 1)
    pick = jnp.where((lane >= row * per) & (lane < (row + 1) * per), 1.0, 0.0).astype(bf16)
    lhs = jnp.concatenate(split(v, parts), axis=1)
    rhs = jnp.concatenate([pick] * parts, axis=0)
    return jnp.dot(lhs, rhs, preferred_element_type=f32)


def group_lanes(states, heads_here):
    start = (lax.axis_index("head") * heads_here) // (H // G)
    return pl.ds(pl.multiple_of(start * states, states), states)


def as_column(row):
    n = row.shape[1]
    wide = jnp.broadcast_to(row, (n, n))
    here = lax.broadcasted_iota(jnp.int32, (n, n), 0) == lax.broadcasted_iota(jnp.int32, (n, n), 1)
    return jnp.sum(jnp.where(here, wide, 0.0), axis=1, keepdims=True)


def widen_columns(v, width, parts):
    heads = v.shape[0]
    per = width // heads
    row = lax.broadcasted_iota(jnp.int32, (heads, width), 0)
    lane = lax.broadcasted_iota(jnp.int32, (heads, width), 1)
    pick = jnp.where((lane >= row * per) & (lane < (row + 1) * per), 1.0, 0.0).astype(bf16)
    lhs = jnp.concatenate(split(v, parts), axis=0)
    rhs = jnp.concatenate([pick] * parts, axis=0)
    return lax.dot_general(lhs, rhs, (((0,), (0,)), ((), ())), preferred_element_type=f32)


def state_kernel(
    len_hbm, dt_hbm, a_hbm, bias_hbm, x_hbm, b_hbm, s0_hbm, z_hbm, cp_hbm,
    skip_hbm, gain_hbm, xd_hbm, zd_hbm, bd_hbm, cd_hbm, dtd_hbm,
    fs_ref, c_ref, r_ref, valid_ref, x_ref, b_ref, s0_ref, z_ref, cp_ref,
    skip_ref, gain_ref, xd_ref, zd_ref, bd_ref, cd_ref, dtd_ref, a_ref, bias_ref,
    len_ref, dt_ref, sems,
):
    heads, length = dt_ref.shape
    width = x_ref.shape[1]
    states = s0_ref.shape[0]
    lanes = group_lanes(states, heads)
    copies = [
        pltpu.make_async_copy(source, target, sems.at[i])
        for i, (source, target) in enumerate((
            (len_hbm, len_ref), (dt_hbm, dt_ref), (a_hbm, a_ref), (bias_hbm, bias_ref),
            (x_hbm, x_ref), (b_hbm.at[:, lanes], b_ref), (s0_hbm, s0_ref),
            (z_hbm, z_ref), (cp_hbm.at[:, lanes], cp_ref), (skip_hbm, skip_ref),
            (gain_hbm, gain_ref), (xd_hbm, xd_ref), (zd_hbm, zd_ref),
            (bd_hbm.at[:, lanes], bd_ref), (cd_hbm.at[:, lanes], cd_ref), (dtd_hbm, dtd_ref),
        ))
    ]
    for copy in copies:
        copy.start()
    row = lax.broadcasted_iota(jnp.int32, (length, length), 0)
    lane = lax.broadcasted_iota(jnp.int32, (length, length), 1)
    upper = jnp.where(row <= lane, 1.0, 0.0).astype(bf16)
    for copy in copies[:4]:
        copy.wait()
    valid = lax.broadcasted_iota(jnp.int32, (heads, length), 1) < len_ref[0]
    delta = jnp.where(valid, softplus(dt_ref[...] + as_column(bias_ref[...])), 0.0)
    rate = delta * as_column(a_ref[...]) * (-LOG2E)
    sums = jnp.dot(
        jnp.concatenate(split(rate, 3), axis=1),
        jnp.concatenate([upper] * 3, axis=0),
        preferred_element_type=f32,
    )
    rows = lax.broadcasted_iota(jnp.int32, valid_ref.shape, 0)
    valid_ref[...] = jnp.where(rows < len_ref[0], 1.0, 0.0)
    c_ref[...] = sums.T
    r_ref[...] = jnp.log2(delta) - sums
    last = sums[:, length - 1 :]
    weight = jnp.exp2(last - sums) * delta
    total = widen_columns(jnp.broadcast_to(jnp.exp2(last), (heads, 8)), width, 2)[0:1, :]
    wide = widen_columns(weight, width, 2)
    copies[4].wait()
    copies[5].wait()
    xw = (x_ref[...].astype(f32) * wide).astype(bf16)
    fresh = lax.dot_general(b_ref[...], xw, (((0,), (0,)), ((), ())), preferred_element_type=f32)
    copies[6].wait()
    fs_ref[...] = (fresh + total * s0_ref[...]).astype(bf16)
    for copy in copies[7:]:
        copy.wait()


def read_kernel(*refs):
    n = (len(refs) - 1) // 2
    fs_ref = refs[0]
    states, width = fs_ref.shape
    heads = width // 64
    me = lax.axis_index("sample")
    lanes = group_lanes(states, heads)
    rows = []
    for k in range(n):
        block = refs[1 + k][:, lanes].astype(f32)
        mine = lax.broadcasted_iota(jnp.int32, block.shape, 0) == me
        rows.append(jnp.sum(jnp.where(mine, block, 0.0), axis=0, keepdims=True))
    q = jnp.concatenate(rows, axis=0).astype(bf16)
    reads = jnp.dot(q, fs_ref[...], preferred_element_type=f32)
    for k in range(n):
        refs[1 + n + k][...] = reads[k : k + 1, :]


def prompt_kernel(
    fs_ref, x_ref, z_ref, b_ref, cp_ref, s0_ref, c_ref, r_ref, skip_ref, gain_ref,
    xd_ref, zd_ref, bd_ref, cd_ref, dtd_ref, a_ref, bias_ref,
    gated_ref, sq_ref, u_ref, v_ref, fs_hbm, m_ref, sem,
):
    length, heads = c_ref.shape
    _, width = s0_ref.shape
    per = width // heads
    prompts = xd_ref.shape[0]
    store = pltpu.make_async_copy(fs_ref, fs_hbm, sem)
    store.start()
    cp = cp_ref[...]
    scores = lax.dot_general(cp, b_ref[...], (((1,), (1,)), ((), ())), preferred_element_type=f32)
    row = lax.broadcasted_iota(jnp.int32, (length, length), 0)
    lane = lax.broadcasted_iota(jnp.int32, (length, length), 1)
    scores = jnp.where(row >= lane, scores, 0.0)
    m_ref[...] = jnp.dot(cp, s0_ref[...].astype(bf16), preferred_element_type=f32)

    step = softplus(dtd_ref[...] + bias_ref[...])
    cb = cd_ref[...].astype(f32) * bd_ref[...].astype(f32)
    cb = jnp.sum(cb, axis=1, keepdims=True)
    gain = step * cb + skip_ref[...]
    skips = jnp.broadcast_to(skip_ref[...], (8, heads))
    wide = widen(jnp.concatenate([jnp.exp(-step * a_ref[...]), gain], axis=0), width, 3)
    skip = widen(skips, width, 3)[0:1, :]
    gate = silu(zd_ref[...].astype(f32))
    u_ref[...] = wide[:prompts] * gate
    v_ref[...] = wide[prompts:] * xd_ref[...].astype(f32) * gate

    rt = r_ref[...]
    c = c_ref[...]
    pair = 2 * per
    low = lax.broadcasted_iota(jnp.int32, (length, pair), 1) < per
    squares = jnp.zeros((length, pair), f32)
    for q in range(heads // 2):
        ch = slice(q * pair, (q + 1) * pair)
        x = x_ref[:, ch]
        xf = x.astype(f32)
        x_cat = jnp.concatenate(
            [jnp.where(low, xf, 0.0).astype(bf16), jnp.where(low, 0.0, xf).astype(bf16)], axis=0
        )
        parts = []
        cols = []
        for h in (2 * q, 2 * q + 1):
            col = jnp.broadcast_to(c[:, h : h + 1], (length, length))
            arg = jnp.minimum(col + rt[h : h + 1, :], CAP)
            parts.append((jnp.exp2(arg) * scores).astype(bf16))
            cols.append(col)
        y = jnp.dot(jnp.concatenate(parts, axis=1), x_cat, preferred_element_type=f32)
        decay = jnp.exp2(jnp.where(low, cols[0], cols[1]))
        y = y + decay * m_ref[:, ch] + skip[:, ch] * xf
        gated = y * silu(z_ref[:, ch].astype(f32))
        gated_ref[:, ch] = gated * gain_ref[:, ch]
        squares = squares + gated * gated
    total = jnp.broadcast_to(jnp.sum(squares, axis=1, keepdims=True), (length, length))
    sq_ref[...] = total.T[0:1, :]
    store.wait()


def slot_kernel(*refs):
    sq_ref, u_ref, v_ref = refs[:3]
    read_refs = refs[3:-2]
    gated_ref, pay_ref = refs[-2:]
    prompts, width = u_ref.shape
    me = lax.axis_index("sample")
    prompt = lax.broadcasted_iota(jnp.int32, (prompts, width), 0)
    reads = jnp.zeros((prompts, width), f32)
    for k, ref in enumerate(read_refs):
        reads = jnp.where(prompt == (me ^ k), ref[...], reads)
    gated = u_ref[...] * reads + v_ref[...]
    gated_ref[...] = gated
    total = jnp.broadcast_to(jnp.sum(gated * gated, axis=1, keepdims=True), (prompts, 128))
    row = lax.broadcasted_iota(jnp.int32, (prompts, 128), 0)
    lane = lax.broadcasted_iota(jnp.int32, (prompts, 128), 1)
    pay_ref[0:1, :] = sq_ref[...]
    pay_ref[1:2, :] = jnp.sum(jnp.where(row == lane, total, 0.0), axis=0, keepdims=True)


def norm_kernel(*refs, channels, payloads):
    valid_ref, gated_ref, dec_ref, gain_ref = refs[:4]
    pay_refs = refs[4 : 4 + payloads]
    out_hbm, dec_hbm, out_ref, out_dec_ref, sems = refs[4 + payloads :]
    length = gated_ref.shape[0]
    prompts = dec_ref.shape[0]
    total = pay_refs[0][...]
    for ref in pay_refs[1:]:
        total = total + ref[...]
    scale = lax.rsqrt(total * (1.0 / channels) + epsilon)
    row = lax.broadcasted_iota(jnp.int32, (prompts, 128), 0)
    lane = lax.broadcasted_iota(jnp.int32, (prompts, 128), 1)
    wide = jnp.broadcast_to(scale[1:2, :], (prompts, 128))
    dec = jnp.sum(jnp.where(row == lane, wide, 0.0), axis=1, keepdims=True)
    out_dec_ref[...] = (dec_ref[...] * dec * gain_ref[...]).astype(bf16)
    copies = [pltpu.make_async_copy(out_dec_ref, dec_hbm, sems.at[0])]
    copies[0].start()
    column = jnp.broadcast_to(scale[0:1, :], (length, length)).T * valid_ref[...]
    column = column[:, 0:1]
    for i in range(CHUNKS):
        rows = slice(i * length // CHUNKS, (i + 1) * length // CHUNKS)
        out_ref[rows, :] = (gated_ref[rows, :] * column[rows, :]).astype(bf16)
        copies.append(
            pltpu.make_async_copy(out_ref.at[rows, :], out_hbm.at[rows, :], sems.at[1 + i])
        )
        copies[-1].start()
    for copy in copies:
        copy.wait()


VMEM = pltpu.MemorySpace.VMEM
HBM = pltpu.MemorySpace.HBM


def call(kernel, ins, outs, scratch=(), far=(), fetch=False):
    space = HBM if fetch else VMEM
    outs = [(VMEM, *out) for out in outs] + [(HBM, *out) for out in far]
    return pl.pallas_call(
        kernel,
        in_specs=[pl.BlockSpec(memory_space=pl.ANY if v.size == 1 else space) for v in ins],
        out_specs=tuple(pl.BlockSpec(memory_space=out[0]) for out in outs),
        out_shape=tuple(out[0](*out[1:]) for out in outs),
        scratch_shapes=list(scratch),
        compiler_params=pltpu.CompilerParams(vmem_limit_bytes=GRANT),
    )(*(v if v.size == 1 else pltpu.with_memory_space_constraint(v, space) for v in ins))


def make_body(mesh):
    samples = mesh.shape["sample"]
    head_parts = mesh.shape["head"]

    def swap(v, axis, k):
        return lax.ppermute(v, axis, [(i, i ^ k) for i in range(mesh.shape[axis])])

    def body(
        x_pre, z_pre, b_pre, c_pre, dt_pre, lengths, init_state, a_rates, dt_bias, skip_scale,
        norm_gain, x_dec, z_dec, b_dec, c_dec, dt_dec,
    ):
        return layer(
            x_pre, z_pre, b_pre, c_pre, dt_pre, lengths, init_state, a_rates, dt_bias,
            skip_scale, norm_gain, x_dec, z_dec, b_dec, c_dec, dt_dec,
        )

    def layer(
        x_pre, z_pre, b_pre, c_pre, dt_pre, lengths, init_state, a_rates, dt_bias, skip_scale,
        norm_gain, x_dec, z_dec, b_dec, c_dec, dt_dec,
    ):
        length, width = x_pre.shape[1:]
        states = init_state.shape[1]
        heads = a_rates.shape[0]
        prompts = x_dec.shape[1]
        x, z, b, cp, dt, s0 = (v[0] for v in (x_pre, z_pre, b_pre, c_pre, dt_pre, init_state))
        xd, zd, bd, cd, dtd = (v[0] for v in (x_dec, z_dec, b_dec, c_dec, dt_dec))
        a, bias, skip, gain = (v[None] for v in (a_rates, dt_bias, skip_scale, norm_gain))
        queries = [cd] + [swap(cd, "sample", k) for k in range(1, samples)]
        fs, c, r, valid, *loaded = call(
            state_kernel,
            (lengths, dt.T, a, bias, x, b, s0, z, cp, skip, gain, xd, zd, bd, cd, dtd),
            (
                ((states, width), bf16), ((length, heads), f32), ((heads, length), f32),
                ((length, 128), f32), ((length, width), bf16), ((length, states), bf16), ((states, width), f32),
                ((length, width), bf16), ((length, states), bf16),
                ((1, heads), f32), ((1, width), f32),
                ((prompts, width), bf16), ((prompts, width), bf16),
                ((prompts, states), bf16), ((prompts, states), bf16),
                ((prompts, heads), f32), ((1, heads), f32), ((1, heads), f32),
            ),
            (
                pltpu.SMEM((1,), jnp.int32), pltpu.VMEM((heads, length), f32),
                pltpu.SemaphoreType.DMA((16,)),
            ), fetch=True,
        )
        x, b, s0, z, cp, skip, gain, xd, zd, bd, own, dtd, a, bias = loaded
        reads = call(read_kernel, (fs, *queries), (((1, width), f32),) * samples)
        reads = [reads[0]] + [swap(reads[k], "sample", k) for k in range(1, samples)]
        gated, sq, u, v, fs = call(
            prompt_kernel,
            (fs, x, z, b, cp, s0, c, r, skip, gain, xd, zd, bd, own, dtd, a, bias),
            (((length, width), f32), ((1, length), f32)) + (((prompts, width), f32),) * 2,
            (pltpu.VMEM((length, width), f32), pltpu.SemaphoreType.DMA(())),
            (((states, width), bf16),),
        )
        gated_dec, pay = call(
            slot_kernel, (sq, u, v, *reads), (((prompts, width), f32), ((2, 128), f32))
        )
        pays = [pay] + [swap(pay, "head", k) for k in range(1, head_parts)]
        out_pre, out_dec = call(
            functools.partial(norm_kernel, channels=width * head_parts, payloads=head_parts),
            (valid, gated, gated_dec, gain, *pays), (),
            (
                pltpu.VMEM((length, width), bf16), pltpu.VMEM((prompts, width), bf16),
                pltpu.SemaphoreType.DMA((1 + CHUNKS,)),
            ), (((length, width), bf16), ((prompts, width), bf16)),
        )
        return out_pre[None], fs[None], out_dec[None]

    return body


def solution(mesh):
    tokens = P(("rep", "sample"), None, "head")
    groups = P(("rep", "sample"), None, None)
    in_specs = (
        tokens, tokens, groups, groups, tokens, P(("rep", "sample")), tokens,
        P("head"), P("head"), P("head"), P("head"), tokens, tokens, groups, groups, tokens,
    )
    return jax.shard_map(
        make_body(mesh), mesh=mesh, in_specs=in_specs, out_specs=(tokens,) * 3, check_vma=False
    )
```

```python
import functools

import jax
import jax.numpy as jnp
from jax import lax
from jax.experimental import pallas as pl
from jax.experimental.pallas import tpu as pltpu
from jax.sharding import PartitionSpec as P


H = 128
G = 4
epsilon = 1e-05
f32 = jnp.float32
bf16 = jnp.bfloat16
LOG2E = 1.4426950408889634
CAP = 100.0
CHUNKS = 4
GRANT = 16 << 20


def softplus(v):
    return jnp.maximum(v, 0.0) + jnp.log1p(jnp.exp(-jnp.abs(v)))


def silu(z):
    half = 0.5 * z
    return half * (1.0 + jnp.tanh(half))


def split(v, parts):
    out = []
    for _ in range(parts):
        piece = v.astype(bf16)
        out.append(piece)
        v = v - piece.astype(f32)
    return out


def widen(v, width, parts):
    heads = v.shape[1]
    per = width // heads
    row = lax.broadcasted_iota(jnp.int32, (heads, width), 0)
    lane = lax.broadcasted_iota(jnp.int32, (heads, width), 1)
    pick = jnp.where((lane >= row * per) & (lane < (row + 1) * per), 1.0, 0.0).astype(bf16)
    lhs = jnp.concatenate(split(v, parts), axis=1)
    rhs = jnp.concatenate([pick] * parts, axis=0)
    return jnp.dot(lhs, rhs, preferred_element_type=f32)


def group_lanes(states, heads_here):
    start = (lax.axis_index("head") * heads_here) // (H // G)
    return pl.ds(pl.multiple_of(start * states, states), states)


def as_column(row):
    n = row.shape[1]
    wide = jnp.broadcast_to(row, (n, n))
    here = lax.broadcasted_iota(jnp.int32, (n, n), 0) == lax.broadcasted_iota(jnp.int32, (n, n), 1)
    return jnp.sum(jnp.where(here, wide, 0.0), axis=1, keepdims=True)


def widen_columns(v, width, parts):
    heads = v.shape[0]
    per = width // heads
    row = lax.broadcasted_iota(jnp.int32, (heads, width), 0)
    lane = lax.broadcasted_iota(jnp.int32, (heads, width), 1)
    pick = jnp.where((lane >= row * per) & (lane < (row + 1) * per), 1.0, 0.0).astype(bf16)
    lhs = jnp.concatenate(split(v, parts), axis=0)
    rhs = jnp.concatenate([pick] * parts, axis=0)
    return lax.dot_general(lhs, rhs, (((0,), (0,)), ((), ())), preferred_element_type=f32)


def state_kernel(
    len_hbm, dt_hbm, a_hbm, bias_hbm, x_hbm, b_hbm, s0_hbm, z_hbm, cp_hbm,
    skip_hbm, gain_hbm, xd_hbm, zd_hbm, bd_hbm, cd_hbm, dtd_hbm,
    fs_ref, c_ref, r_ref, valid_ref, x_ref, b_ref, s0_ref, z_ref, cp_ref,
    skip_ref, gain_ref, xd_ref, zd_ref, bd_ref, cd_ref, dtd_ref, a_ref, bias_ref,
    len_ref, dt_ref, sems,
):
    heads, length = dt_ref.shape
    width = x_ref.shape[1]
    states = s0_ref.shape[0]
    lanes = group_lanes(states, heads)
    copies = [
        pltpu.make_async_copy(source, target, sems.at[i])
        for i, (source, target) in enumerate((
            (len_hbm, len_ref), (dt_hbm, dt_ref), (a_hbm, a_ref), (bias_hbm, bias_ref),
            (x_hbm, x_ref), (b_hbm.at[:, lanes], b_ref), (s0_hbm, s0_ref),
            (z_hbm, z_ref), (cp_hbm.at[:, lanes], cp_ref), (skip_hbm, skip_ref),
            (gain_hbm, gain_ref), (xd_hbm, xd_ref), (zd_hbm, zd_ref),
            (bd_hbm.at[:, lanes], bd_ref), (cd_hbm.at[:, lanes], cd_ref), (dtd_hbm, dtd_ref),
        ))
    ]
    for copy in copies:
        copy.start()
    row = lax.broadcasted_iota(jnp.int32, (length, length), 0)
    lane = lax.broadcasted_iota(jnp.int32, (length, length), 1)
    upper = jnp.where(row <= lane, 1.0, 0.0).astype(bf16)
    for copy in copies[:4]:
        copy.wait()
    valid = lax.broadcasted_iota(jnp.int32, (heads, length), 1) < len_ref[0]
    delta = jnp.where(valid, softplus(dt_ref[...] + as_column(bias_ref[...])), 0.0)
    rate = delta * as_column(a_ref[...]) * (-LOG2E)
    sums = jnp.dot(
        jnp.concatenate(split(rate, 3), axis=1),
        jnp.concatenate([upper] * 3, axis=0),
        preferred_element_type=f32,
    )
    rows = lax.broadcasted_iota(jnp.int32, valid_ref.shape, 0)
    valid_ref[...] = jnp.where(rows < len_ref[0], 1.0, 0.0)
    c_ref[...] = sums.T
    r_ref[...] = jnp.log2(delta) - sums
    last = sums[:, length - 1 :]
    weight = jnp.exp2(last - sums) * delta
    total = widen_columns(jnp.broadcast_to(jnp.exp2(last), (heads, 8)), width, 2)[0:1, :]
    wide = widen_columns(weight, width, 2)
    copies[4].wait()
    copies[5].wait()
    xw = (x_ref[...].astype(f32) * wide).astype(bf16)
    fresh = lax.dot_general(b_ref[...], xw, (((0,), (0,)), ((), ())), preferred_element_type=f32)
    copies[6].wait()
    fs_ref[...] = (fresh + total * s0_ref[...]).astype(bf16)
    for copy in copies[7:]:
        copy.wait()


def entry(table, index):
    value = jnp.int32(table[0])
    for i, number in enumerate(table[1:], 1):
        value = jnp.where(index == i, jnp.int32(number), value)
    return value


def read_kernel(*refs, asks, answers):
    fs_ref, own_ref = refs[:2]
    ask_refs = refs[2 : 2 + len(asks)]
    mine_ref = refs[2 + len(asks)]
    out_refs = refs[3 + len(asks) :]
    states, width = fs_ref.shape
    me = lax.axis_index("sample")
    lanes = pl.ds(0, states)
    if own_ref.shape[1] != states:
        lanes = group_lanes(states, width // 64)
    n = own_ref.shape[0]
    row = lax.broadcasted_iota(jnp.int32, (n, states), 0)
    q = jnp.zeros((n, states), f32)
    for who, ref in [(me, own_ref)] + [(entry(t, me), r) for t, r in zip(asks, ask_refs)]:
        block = ref[:, lanes].astype(f32)
        query = jnp.sum(jnp.where(row == me, block, 0.0), axis=0, keepdims=True)
        q = jnp.where(row == who, query, q)
    reads = jnp.dot(q.astype(bf16), fs_ref[...], preferred_element_type=f32)
    slot = lax.broadcasted_iota(jnp.int32, (n, width), 0)
    for who, ref in [(me, mine_ref)] + [(entry(t, me), r) for t, r in zip(answers, out_refs)]:
        ref[...] = jnp.sum(jnp.where(slot == who, reads, 0.0), axis=0, keepdims=True)


def prompt_kernel(
    fs_ref, x_ref, z_ref, b_ref, cp_ref, s0_ref, c_ref, r_ref, skip_ref, gain_ref,
    xd_ref, zd_ref, bd_ref, cd_ref, dtd_ref, a_ref, bias_ref,
    gated_ref, sq_ref, u_ref, v_ref, fs_hbm, m_ref, sem,
):
    length, heads = c_ref.shape
    _, width = s0_ref.shape
    per = width // heads
    prompts = xd_ref.shape[0]
    store = pltpu.make_async_copy(fs_ref, fs_hbm, sem)
    store.start()
    cp = cp_ref[...]
    scores = lax.dot_general(cp, b_ref[...], (((1,), (1,)), ((), ())), preferred_element_type=f32)
    row = lax.broadcasted_iota(jnp.int32, (length, length), 0)
    lane = lax.broadcasted_iota(jnp.int32, (length, length), 1)
    scores = jnp.where(row >= lane, scores, 0.0)
    m_ref[...] = jnp.dot(cp, s0_ref[...].astype(bf16), preferred_element_type=f32)

    step = softplus(dtd_ref[...] + bias_ref[...])
    cb = cd_ref[...].astype(f32) * bd_ref[...].astype(f32)
    cb = jnp.sum(cb, axis=1, keepdims=True)
    gain = step * cb + skip_ref[...]
    skips = jnp.broadcast_to(skip_ref[...], (8, heads))
    wide = widen(jnp.concatenate([jnp.exp(-step * a_ref[...]), gain], axis=0), width, 3)
    skip = widen(skips, width, 3)[0:1, :]
    gate = silu(zd_ref[...].astype(f32))
    u_ref[...] = wide[:prompts] * gate
    v_ref[...] = wide[prompts:] * xd_ref[...].astype(f32) * gate

    rt = r_ref[...]
    c = c_ref[...]
    pair = 2 * per
    low = lax.broadcasted_iota(jnp.int32, (length, pair), 1) < per
    squares = jnp.zeros((length, pair), f32)
    for q in range(heads // 2):
        ch = slice(q * pair, (q + 1) * pair)
        x = x_ref[:, ch]
        xf = x.astype(f32)
        x_cat = jnp.concatenate(
            [jnp.where(low, xf, 0.0).astype(bf16), jnp.where(low, 0.0, xf).astype(bf16)], axis=0
        )
        parts = []
        cols = []
        for h in (2 * q, 2 * q + 1):
            col = jnp.broadcast_to(c[:, h : h + 1], (length, length))
            arg = jnp.minimum(col + rt[h : h + 1, :], CAP)
            parts.append((jnp.exp2(arg) * scores).astype(bf16))
            cols.append(col)
        y = jnp.dot(jnp.concatenate(parts, axis=1), x_cat, preferred_element_type=f32)
        decay = jnp.exp2(jnp.where(low, cols[0], cols[1]))
        y = y + decay * m_ref[:, ch] + skip[:, ch] * xf
        gated = y * silu(z_ref[:, ch].astype(f32))
        gated_ref[:, ch] = gated * gain_ref[:, ch]
        squares = squares + gated * gated
    total = jnp.broadcast_to(jnp.sum(squares, axis=1, keepdims=True), (length, length))
    sq_ref[...] = total.T[0:1, :]
    store.wait()


def slot_kernel(*refs, sources):
    sq_ref, u_ref, v_ref = refs[:3]
    read_refs = refs[3:-2]
    gated_ref, pay_ref = refs[-2:]
    prompts, width = u_ref.shape
    me = lax.axis_index("sample")
    prompt = lax.broadcasted_iota(jnp.int32, (prompts, width), 0)
    reads = jnp.zeros((prompts, width), f32)
    whose = [me] + [entry(table, me) for table in sources]
    for who, ref in zip(whose, read_refs):
        reads = jnp.where(prompt == who, ref[...], reads)
    gated = u_ref[...] * reads + v_ref[...]
    gated_ref[...] = gated
    total = jnp.broadcast_to(jnp.sum(gated * gated, axis=1, keepdims=True), (prompts, 128))
    row = lax.broadcasted_iota(jnp.int32, (prompts, 128), 0)
    lane = lax.broadcasted_iota(jnp.int32, (prompts, 128), 1)
    pay_ref[0:1, :] = sq_ref[...]
    pay_ref[1:2, :] = jnp.sum(jnp.where(row == lane, total, 0.0), axis=0, keepdims=True)


def norm_kernel(*refs, channels, payloads):
    valid_ref, gated_ref, dec_ref, gain_ref = refs[:4]
    pay_refs = refs[4 : 4 + payloads]
    out_hbm, dec_hbm, out_ref, out_dec_ref, sems = refs[4 + payloads :]
    length = gated_ref.shape[0]
    prompts = dec_ref.shape[0]
    total = pay_refs[0][...]
    for ref in pay_refs[1:]:
        total = total + ref[...]
    scale = lax.rsqrt(total * (1.0 / channels) + epsilon)
    row = lax.broadcasted_iota(jnp.int32, (prompts, 128), 0)
    lane = lax.broadcasted_iota(jnp.int32, (prompts, 128), 1)
    wide = jnp.broadcast_to(scale[1:2, :], (prompts, 128))
    dec = jnp.sum(jnp.where(row == lane, wide, 0.0), axis=1, keepdims=True)
    out_dec_ref[...] = (dec_ref[...] * dec * gain_ref[...]).astype(bf16)
    copies = [pltpu.make_async_copy(out_dec_ref, dec_hbm, sems.at[0])]
    copies[0].start()
    column = jnp.broadcast_to(scale[0:1, :], (length, length)).T * valid_ref[...]
    column = column[:, 0:1]
    for i in range(CHUNKS):
        rows = slice(i * length // CHUNKS, (i + 1) * length // CHUNKS)
        out_ref[rows, :] = (gated_ref[rows, :] * column[rows, :]).astype(bf16)
        copies.append(
            pltpu.make_async_copy(out_ref.at[rows, :], out_hbm.at[rows, :], sems.at[1 + i])
        )
        copies[-1].start()
    for copy in copies:
        copy.wait()


VMEM = pltpu.MemorySpace.VMEM
HBM = pltpu.MemorySpace.HBM


def call(kernel, ins, outs, scratch=(), far=(), fetch=False):
    space = HBM if fetch else VMEM
    outs = [(VMEM, *out) for out in outs] + [(HBM, *out) for out in far]
    return pl.pallas_call(
        kernel,
        in_specs=[pl.BlockSpec(memory_space=pl.ANY if v.size == 1 else space) for v in ins],
        out_specs=tuple(pl.BlockSpec(memory_space=out[0]) for out in outs),
        out_shape=tuple(out[0](*out[1:]) for out in outs),
        scratch_shapes=list(scratch),
        compiler_params=pltpu.CompilerParams(vmem_limit_bytes=GRANT),
    )(*(v if v.size == 1 else pltpu.with_memory_space_constraint(v, space) for v in ins))


SCHEDULES = {
    ("query", 4): [
        [(0, 2), (1, 3), (2, 0), (3, 1)],
        [(0, 3), (1, 2), (2, 1), (3, 0)],
        [(0, 1), (1, 0), (2, 3), (3, 2)],
    ],
    ("reads", 4): [
        [(0, 3), (1, 2), (2, 1), (3, 0)],
        [(0, 2), (1, 3), (2, 0), (3, 1)],
        [(0, 1), (1, 0), (2, 3), (3, 2)],
    ],
}


def steps(tag, n):
    if (tag, n) in SCHEDULES:
        return SCHEDULES[tag, n]
    return [[(i, i ^ k) for i in range(n)] for k in range(n - 1, 0, -1)]


def sources(pairs, n):
    return [dict((b, a) for a, b in pairs).get(i, -1) for i in range(n)]


def targets(pairs, n):
    return [dict(pairs).get(i, -1) for i in range(n)]


def make_body(mesh):
    samples = mesh.shape["sample"]
    head_parts = mesh.shape["head"]

    def body(
        x_pre, z_pre, b_pre, c_pre, dt_pre, lengths, init_state, a_rates, dt_bias, skip_scale,
        norm_gain, x_dec, z_dec, b_dec, c_dec, dt_dec,
    ):
        return layer(
            x_pre, z_pre, b_pre, c_pre, dt_pre, lengths, init_state, a_rates, dt_bias,
            skip_scale, norm_gain, x_dec, z_dec, b_dec, c_dec, dt_dec,
        )

    def layer(
        x_pre, z_pre, b_pre, c_pre, dt_pre, lengths, init_state, a_rates, dt_bias, skip_scale,
        norm_gain, x_dec, z_dec, b_dec, c_dec, dt_dec,
    ):
        length, width = x_pre.shape[1:]
        states = init_state.shape[1]
        heads = a_rates.shape[0]
        prompts = x_dec.shape[1]
        x, z, b, cp, dt, s0 = (v[0] for v in (x_pre, z_pre, b_pre, c_pre, dt_pre, init_state))
        xd, zd, bd, cd, dtd = (v[0] for v in (x_dec, z_dec, b_dec, c_dec, dt_dec))
        a, bias, skip, gain = (v[None] for v in (a_rates, dt_bias, skip_scale, norm_gain))
        asking = steps("query", samples)
        answering = steps("reads", samples)
        queries = [lax.ppermute(cd, "sample", pairs) for pairs in asking]
        fs, c, r, valid, *loaded = call(
            state_kernel,
            (lengths, dt.T, a, bias, x, b, s0, z, cp, skip, gain, xd, zd, bd, cd, dtd),
            (
                ((states, width), bf16), ((length, heads), f32), ((heads, length), f32),
                ((length, 128), f32), ((length, width), bf16), ((length, states), bf16), ((states, width), f32),
                ((length, width), bf16), ((length, states), bf16),
                ((1, heads), f32), ((1, width), f32),
                ((prompts, width), bf16), ((prompts, width), bf16),
                ((prompts, states), bf16), ((prompts, states), bf16),
                ((prompts, heads), f32), ((1, heads), f32), ((1, heads), f32),
            ),
            (
                pltpu.SMEM((1,), jnp.int32), pltpu.VMEM((heads, length), f32),
                pltpu.SemaphoreType.DMA((16,)),
            ), fetch=True,
        )
        x, b, s0, z, cp, skip, gain, xd, zd, bd, own, dtd, a, bias = loaded
        reads = call(
            functools.partial(
                read_kernel, asks=[sources(pairs, samples) for pairs in asking],
                answers=[targets(pairs, samples) for pairs in answering],
            ), (fs, cd, *queries), (((1, width), f32),) * (1 + len(answering)),
        )
        reads = [reads[0]] + [
            lax.ppermute(v, "sample", pairs)
            for v, pairs in zip(reads[1:], answering)
        ]
        gated, sq, u, v, fs = call(
            prompt_kernel,
            (fs, x, z, b, cp, s0, c, r, skip, gain, xd, zd, bd, own, dtd, a, bias),
            (((length, width), f32), ((1, length), f32)) + (((prompts, width), f32),) * 2,
            (pltpu.VMEM((length, width), f32), pltpu.SemaphoreType.DMA(())),
            (((states, width), bf16),),
        )
        gated_dec, pay = call(
            functools.partial(
                slot_kernel, sources=[sources(pairs, samples) for pairs in answering]
            ), (sq, u, v, *reads), (((prompts, width), f32), ((2, 128), f32)),
        )
        pays = [pay] + [lax.ppermute(pay, "head", pairs) for pairs in steps("sums", head_parts)]
        out_pre, out_dec = call(
            functools.partial(norm_kernel, channels=width * head_parts, payloads=head_parts),
            (valid, gated, gated_dec, gain, *pays), (),
            (
                pltpu.VMEM((length, width), bf16), pltpu.VMEM((prompts, width), bf16),
                pltpu.SemaphoreType.DMA((1 + CHUNKS,)),
            ), (((length, width), bf16), ((prompts, width), bf16)),
        )
        return out_pre[None], fs[None], out_dec[None]

    return body


def solution(mesh):
    tokens = P(("rep", "sample"), None, "head")
    groups = P(("rep", "sample"), None, None)
    in_specs = (
        tokens, tokens, groups, groups, tokens, P(("rep", "sample")), tokens,
        P("head"), P("head"), P("head"), P("head"), tokens, tokens, groups, groups, tokens,
    )
    return jax.shard_map(
        make_body(mesh), mesh=mesh, in_specs=in_specs, out_specs=(tokens,) * 3, check_vma=False
    )
```

```python
import functools

import jax
import jax.numpy as jnp
from jax import lax
from jax.experimental import pallas as pl
from jax.experimental.pallas import tpu as pltpu
from jax.sharding import PartitionSpec as P


H = 128
G = 4
epsilon = 1e-05
f32 = jnp.float32
bf16 = jnp.bfloat16
LOG2E = 1.4426950408889634
CAP = 100.0
CHUNKS = 4
GRANT = 16 << 20


def softplus(v):
    return jnp.maximum(v, 0.0) + jnp.log1p(jnp.exp(-jnp.abs(v)))


def silu(z):
    half = 0.5 * z
    return half * (1.0 + jnp.tanh(half))


def split(v, parts):
    out = []
    for _ in range(parts):
        piece = v.astype(bf16)
        out.append(piece)
        v = v - piece.astype(f32)
    return out


def picks(heads, width, parts):
    per = width // heads
    row = lax.broadcasted_iota(jnp.int32, (heads, width), 0)
    lane = lax.broadcasted_iota(jnp.int32, (heads, width), 1)
    pick = jnp.where((lane >= row * per) & (lane < (row + 1) * per), 1.0, 0.0).astype(bf16)
    return jnp.concatenate([pick] * parts, axis=0)


def widen(v, width, parts):
    lhs = jnp.concatenate(split(v, parts), axis=1)
    return jnp.dot(lhs, picks(v.shape[1], width, parts), preferred_element_type=f32)


def as_column(row):
    n = row.shape[1]
    wide = jnp.broadcast_to(row, (n, n))
    here = lax.broadcasted_iota(jnp.int32, (n, n), 0) == lax.broadcasted_iota(jnp.int32, (n, n), 1)
    return jnp.sum(jnp.where(here, wide, 0.0), axis=1, keepdims=True)


def widen_columns(v, pick_ref):
    lhs = jnp.concatenate(split(v, pick_ref.shape[0] // v.shape[0]), axis=0)
    return lax.dot_general(
        lhs, pick_ref[...], (((0,), (0,)), ((), ())), preferred_element_type=f32
    )


def group_lanes(states, heads_here):
    start = (lax.axis_index("head") * heads_here) // (H // G)
    return pl.ds(pl.multiple_of(start * states, states), states)


def state_kernel(
    valid_ref, dt_hbm, a_hbm, bias_hbm, x_hbm, b_hbm, s0_hbm,
    fs_ref, sums_ref, delta_ref, x_ref, b_ref, s0_ref, a_ref, bias_ref,
    dt_ref, pick_ref, fresh_ref, sems,
):
    heads, length = dt_ref.shape
    width = x_ref.shape[1]
    states = s0_ref.shape[0]
    lanes = group_lanes(states, heads)
    copies = [
        pltpu.make_async_copy(source, target, sems.at[i])
        for i, (source, target) in enumerate((
            (dt_hbm, dt_ref), (a_hbm, a_ref), (bias_hbm, bias_ref),
            (x_hbm, x_ref), (b_hbm.at[:, lanes], b_ref), (s0_hbm, s0_ref),
        ))
    ]
    for copy in copies:
        copy.start()
    row = lax.broadcasted_iota(jnp.int32, (length, length), 0)
    lane = lax.broadcasted_iota(jnp.int32, (length, length), 1)
    upper = jnp.where(row <= lane, 1.0, 0.0).astype(bf16)
    pick_ref[...] = picks(heads, width, 2)
    for copy in copies[:3]:
        copy.wait()
    delta = softplus(dt_ref[...] + as_column(bias_ref[...])) * valid_ref[...]
    rate = delta * as_column(a_ref[...]) * (-LOG2E)
    sums = jnp.dot(
        jnp.concatenate(split(rate, 3), axis=1),
        jnp.concatenate([upper] * 3, axis=0),
        preferred_element_type=f32,
    )
    sums_ref[...] = sums
    delta_ref[...] = delta
    last = sums[:, length - 1 :]
    weight = jnp.exp2(last - sums) * delta
    total = widen_columns(jnp.broadcast_to(jnp.exp2(last), (heads, 8)), pick_ref)[0:1, :]
    wide = widen_columns(weight, pick_ref)
    copies[3].wait()
    copies[4].wait()
    xw = (x_ref[...].astype(f32) * wide).astype(bf16)
    fresh = lax.dot_general(b_ref[...], xw, (((0,), (0,)), ((), ())), preferred_element_type=f32)
    fresh_ref[...] = fresh
    copies[5].wait()
    for i in range(8):
        rows = slice(i * states // 8, (i + 1) * states // 8)
        fs_ref[rows, :] = (fresh_ref[rows, :] + total * s0_ref[rows, :]).astype(bf16)


def read_kernel(fs_ref, query_ref, out_ref):
    states, width = fs_ref.shape
    me = lax.axis_index("sample")
    block = query_ref[:, group_lanes(states, width // 64)].astype(f32)
    mine = lax.broadcasted_iota(jnp.int32, block.shape, 0) == me
    query = jnp.sum(jnp.where(mine, block, 0.0), axis=0, keepdims=True).astype(bf16)
    out_ref[...] = jnp.dot(query, fs_ref[...], preferred_element_type=f32)


def prompt_kernel(
    fs_ref, x_ref, z_ref, b_ref, cp_ref, s0_ref, sums_ref, delta_ref, skip_ref, gain_ref,
    xd_ref, zd_ref, bd_ref, cd_ref, dtd_ref, a_ref, bias_ref,
    gated_ref, sq_ref, u_ref, v_ref, own_ref, fs_hbm, m_ref, sem,
):
    heads, length = sums_ref.shape
    states, width = s0_ref.shape
    per = width // heads
    prompts = xd_ref.shape[0]
    store = pltpu.make_async_copy(fs_ref, fs_hbm, sem)
    store.start()
    lanes = group_lanes(states, heads)
    cp = cp_ref[:, lanes]
    scores = lax.dot_general(cp, b_ref[...], (((1,), (1,)), ((), ())), preferred_element_type=f32)
    row = lax.broadcasted_iota(jnp.int32, (length, length), 0)
    lane = lax.broadcasted_iota(jnp.int32, (length, length), 1)
    scores = jnp.where(row >= lane, scores, 0.0)
    m_ref[...] = jnp.dot(cp, s0_ref[...].astype(bf16), preferred_element_type=f32)

    step = softplus(dtd_ref[...] + bias_ref[...])
    own = cd_ref[:, lanes].astype(f32)
    cb = own * bd_ref[:, lanes].astype(f32)
    cb = jnp.sum(cb, axis=1, keepdims=True)
    gain = step * cb + skip_ref[...]
    skips = jnp.broadcast_to(skip_ref[...], (8, heads))
    wide = widen(jnp.concatenate([jnp.exp(-step * a_ref[...]), gain], axis=0), width, 3)
    skip = widen(skips, width, 3)[0:1, :]
    gate = silu(zd_ref[...].astype(f32))
    u_ref[...] = wide[:prompts] * gate
    v_ref[...] = wide[prompts:] * xd_ref[...].astype(f32) * gate

    mine = lax.broadcasted_iota(jnp.int32, own.shape, 0) == lax.axis_index("sample")
    query = jnp.where(mine, own, 0.0)
    query = jnp.sum(query, axis=0, keepdims=True).astype(bf16)
    own_ref[...] = jnp.dot(query, fs_ref[...], preferred_element_type=f32)

    rt = jnp.log2(delta_ref[...]) - sums_ref[...]
    c = sums_ref[...].T
    pair = 2 * per
    low = lax.broadcasted_iota(jnp.int32, (length, pair), 1) < per
    squares = jnp.zeros((length, pair), f32)
    for q in range(heads // 2):
        ch = slice(q * pair, (q + 1) * pair)
        x = x_ref[:, ch]
        xf = x.astype(f32)
        x_cat = jnp.concatenate(
            [jnp.where(low, xf, 0.0).astype(bf16), jnp.where(low, 0.0, xf).astype(bf16)], axis=0
        )
        parts = []
        cols = []
        for h in (2 * q, 2 * q + 1):
            col = jnp.broadcast_to(c[:, h : h + 1], (length, length))
            arg = jnp.minimum(col + rt[h : h + 1, :], CAP)
            parts.append((jnp.exp2(arg) * scores).astype(bf16))
            cols.append(col)
        y = jnp.dot(jnp.concatenate(parts, axis=1), x_cat, preferred_element_type=f32)
        decay = jnp.exp2(jnp.where(low, cols[0], cols[1]))
        y = y + decay * m_ref[:, ch] + skip[:, ch] * xf
        gated = y * silu(z_ref[:, ch].astype(f32))
        gated_ref[:, ch] = gated * gain_ref[:, ch]
        squares = squares + gated * gated
    total = jnp.broadcast_to(jnp.sum(squares, axis=1, keepdims=True), (length, length))
    sq_ref[...] = total.T[0:1, :]
    store.wait()


def slot_kernel(*refs):
    sq_ref, u_ref, v_ref = refs[:3]
    read_refs = refs[3:-2]
    gated_ref, pay_ref = refs[-2:]
    prompts, width = u_ref.shape
    me = lax.axis_index("sample")
    prompt = lax.broadcasted_iota(jnp.int32, (prompts, width), 0)
    reads = jnp.zeros((prompts, width), f32)
    for k, ref in zip([0] + shifts(prompts), read_refs):
        reads = jnp.where(prompt == lax.rem(me + k, prompts), ref[...], reads)
    gated = u_ref[...] * reads + v_ref[...]
    gated_ref[...] = gated
    total = jnp.broadcast_to(jnp.sum(gated * gated, axis=1, keepdims=True), (prompts, 128))
    row = lax.broadcasted_iota(jnp.int32, (prompts, 128), 0)
    lane = lax.broadcasted_iota(jnp.int32, (prompts, 128), 1)
    pay_ref[0:1, :] = sq_ref[...]
    pay_ref[1:2, :] = jnp.sum(jnp.where(row == lane, total, 0.0), axis=0, keepdims=True)


def norm_kernel(*refs, channels, payloads):
    valid_ref, gated_ref, dec_ref, gain_ref = refs[:4]
    pay_refs = refs[4 : 4 + payloads]
    out_hbm, dec_hbm, out_ref, out_dec_ref, sems = refs[4 + payloads :]
    length = gated_ref.shape[0]
    prompts = dec_ref.shape[0]
    total = pay_refs[0][...]
    for ref in pay_refs[1:]:
        total = total + ref[...]
    scale = lax.rsqrt(total * (1.0 / channels) + epsilon)
    row = lax.broadcasted_iota(jnp.int32, (prompts, 128), 0)
    lane = lax.broadcasted_iota(jnp.int32, (prompts, 128), 1)
    wide = jnp.broadcast_to(scale[1:2, :], (prompts, 128))
    dec = jnp.sum(jnp.where(row == lane, wide, 0.0), axis=1, keepdims=True)
    out_dec_ref[...] = (dec_ref[...] * dec * gain_ref[...]).astype(bf16)
    copies = [pltpu.make_async_copy(out_dec_ref, dec_hbm, sems.at[0])]
    copies[0].start()
    column = jnp.broadcast_to(scale[0:1, :] * valid_ref[...], (length, length)).T[:, 0:1]
    for i in range(CHUNKS):
        rows = slice(i * length // CHUNKS, (i + 1) * length // CHUNKS)
        out_ref[rows, :] = (gated_ref[rows, :] * column[rows, :]).astype(bf16)
        copies.append(
            pltpu.make_async_copy(out_ref.at[rows, :], out_hbm.at[rows, :], sems.at[1 + i])
        )
        copies[-1].start()
    for copy in copies:
        copy.wait()


VMEM = pltpu.MemorySpace.VMEM
HBM = pltpu.MemorySpace.HBM


def call(kernel, ins, outs, scratch=(), far=(), fetch=False):
    spaces = [VMEM if not fetch or i == 0 else HBM for i in range(len(ins))]
    outs = [(VMEM, *out) for out in outs] + [(HBM, *out) for out in far]
    return pl.pallas_call(
        kernel,
        in_specs=[pl.BlockSpec(memory_space=space) for space in spaces],
        out_specs=tuple(pl.BlockSpec(memory_space=out[0]) for out in outs),
        out_shape=tuple(out[0](*out[1:]) for out in outs),
        scratch_shapes=list(scratch),
        compiler_params=pltpu.CompilerParams(vmem_limit_bytes=GRANT),
    )(*(pltpu.with_memory_space_constraint(v, space) for v, space in zip(ins, spaces)))


def shifts(n):
    return [k for j in range(1, n // 2 + 1) for k in dict.fromkeys((j, n - j))]


def make_body(mesh):
    samples = mesh.shape["sample"]
    head_parts = mesh.shape["head"]

    def body(
        x_pre, z_pre, b_pre, c_pre, dt_pre, lengths, init_state, a_rates, dt_bias, skip_scale,
        norm_gain, x_dec, z_dec, b_dec, c_dec, dt_dec,
    ):
        return layer(
            x_pre, z_pre, b_pre, c_pre, dt_pre, lengths, init_state, a_rates, dt_bias,
            skip_scale, norm_gain, x_dec, z_dec, b_dec, c_dec, dt_dec,
        )

    def layer(
        x_pre, z_pre, b_pre, c_pre, dt_pre, lengths, init_state, a_rates, dt_bias, skip_scale,
        norm_gain, x_dec, z_dec, b_dec, c_dec, dt_dec,
    ):
        length, width = x_pre.shape[1:]
        states = init_state.shape[1]
        heads = a_rates.shape[0]
        prompts = x_dec.shape[1]
        x, z, b, cp, dt, s0 = (v[0] for v in (x_pre, z_pre, b_pre, c_pre, dt_pre, init_state))
        xd, zd, bd, cd, dtd = (v[0] for v in (x_dec, z_dec, b_dec, c_dec, dt_dec))
        a, bias, skip, gain = (v[None] for v in (a_rates, dt_bias, skip_scale, norm_gain))

        def shifted(v, k):
            pairs = [(j, (j + k) % samples) for j in range(samples)]
            return lax.ppermute(v, "sample", pairs)

        queries = [shifted(cd, k) for k in shifts(samples)]
        positions = jnp.arange(length, dtype=jnp.int32)
        valid = (positions[None, :] < lengths[:, None]).astype(f32)
        fs, sums, delta, x, b, s0, a, bias = call(
            state_kernel, (valid, dt.T, a, bias, x, b, s0),
            (
                ((states, width), bf16), ((heads, length), f32), ((heads, length), f32),
                ((length, width), bf16), ((length, states), bf16), ((states, width), f32),
                ((1, heads), f32), ((1, heads), f32),
            ),
            (
                pltpu.VMEM((heads, length), f32), pltpu.VMEM((2 * heads, width), bf16),
                pltpu.VMEM((states, width), f32),
                pltpu.SemaphoreType.DMA((6,)),
            ), fetch=True,
        )
        reads = []
        for k, query in zip(shifts(samples), queries):
            (answer,) = call(read_kernel, (fs, query), (((1, width), f32),))
            reads.append(shifted(answer, -k))
        gated, sq, u, v, mine, fs = call(
            prompt_kernel,
            (fs, x, z, b, cp, s0, sums, delta, skip, gain, xd, zd, bd, cd, dtd, a, bias),
            (((length, width), f32), ((1, length), f32)) + (((prompts, width), f32),) * 2
            + (((1, width), f32),),
            (pltpu.VMEM((length, width), f32), pltpu.SemaphoreType.DMA(())),
            (((states, width), bf16),),
        )
        gated_dec, pay = call(
            slot_kernel, (sq, u, v, mine, *reads),
            (((prompts, width), f32), ((2, 128), f32)),
        )
        pays = [pay] + [
            lax.ppermute(pay, "head", [(j, j ^ k) for j in range(head_parts)])
            for k in range(head_parts - 1, 0, -1)
        ]
        out_pre, out_dec = call(
            functools.partial(norm_kernel, channels=width * head_parts, payloads=head_parts),
            (valid, gated, gated_dec, gain, *pays), (),
            (
                pltpu.VMEM((length, width), bf16), pltpu.VMEM((prompts, width), bf16),
                pltpu.SemaphoreType.DMA((1 + CHUNKS,)),
            ), (((length, width), bf16), ((prompts, width), bf16)),
        )
        return out_pre[None], fs[None], out_dec[None]

    return body


def solution(mesh):
    tokens = P(("rep", "sample"), None, "head")
    groups = P(("rep", "sample"), None, None)
    in_specs = (
        tokens, tokens, groups, groups, tokens, P(("rep", "sample")), tokens,
        P("head"), P("head"), P("head"), P("head"), tokens, tokens, groups, groups, tokens,
    )
    return jax.shard_map(
        make_body(mesh), mesh=mesh, in_specs=in_specs, out_specs=(tokens,) * 3, check_vma=False
    )
```

```python
import functools

import jax
import jax.numpy as jnp
from jax import lax
from jax.experimental import pallas as pl
from jax.experimental.pallas import tpu as pltpu
from jax.sharding import PartitionSpec as P


H = 128
G = 4
epsilon = 1e-05
f32 = jnp.float32
bf16 = jnp.bfloat16
LOG2E = 1.4426950408889634
CAP = 100.0
CHUNKS = 4
GRANT = 16 << 20


def softplus(v):
    return jnp.maximum(v, 0.0) + jnp.log1p(jnp.exp(-jnp.abs(v)))


def silu(z):
    half = 0.5 * z
    return half * (1.0 + jnp.tanh(half))


def split(v, parts):
    out = []
    for _ in range(parts):
        piece = v.astype(bf16)
        out.append(piece)
        v = v - piece.astype(f32)
    return out


def picks(heads, width, parts):
    per = width // heads
    row = lax.broadcasted_iota(jnp.int32, (heads, width), 0)
    lane = lax.broadcasted_iota(jnp.int32, (heads, width), 1)
    pick = jnp.where((lane >= row * per) & (lane < (row + 1) * per), 1.0, 0.0).astype(bf16)
    return jnp.concatenate([pick] * parts, axis=0)


def widen(v, width, parts):
    lhs = jnp.concatenate(split(v, parts), axis=1)
    return jnp.dot(lhs, picks(v.shape[1], width, parts), preferred_element_type=f32)


def as_column(row):
    n = row.shape[1]
    wide = jnp.broadcast_to(row, (n, n))
    here = lax.broadcasted_iota(jnp.int32, (n, n), 0) == lax.broadcasted_iota(jnp.int32, (n, n), 1)
    return jnp.sum(jnp.where(here, wide, 0.0), axis=1, keepdims=True)


def widen_columns(v, pick_ref):
    lhs = jnp.concatenate(split(v, pick_ref.shape[0] // v.shape[0]), axis=0)
    return lax.dot_general(
        lhs, pick_ref[...], (((0,), (0,)), ((), ())), preferred_element_type=f32
    )


def widen_row(v, width):
    heads = v.shape[0]
    per = width // heads
    wide = jnp.broadcast_to(v, (heads, 2 * per))
    low = lax.broadcasted_iota(jnp.int32, (1, 2 * per), 1) < per
    rows = [jnp.where(low, wide[i : i + 1], wide[i + 1 : i + 2]) for i in range(0, heads, 2)]
    return jnp.concatenate(rows, axis=1)


def group_lanes(states, heads_here):
    start = (lax.axis_index("head") * heads_here) // (H // G)
    return pl.ds(pl.multiple_of(start * states, states), states)


def state_kernel(
    valid_ref, dt_hbm, a_hbm, bias_hbm, x_hbm, b_hbm, s0_hbm,
    fs_ref, sums_ref, delta_ref, x_ref, b_ref, s0_ref, a_ref, bias_ref,
    dt_ref, pick_ref, fresh_ref, sems,
):
    heads, length = dt_ref.shape
    width = x_ref.shape[1]
    states = s0_ref.shape[0]
    lanes = group_lanes(states, heads)
    copies = [
        pltpu.make_async_copy(source, target, sems.at[i])
        for i, (source, target) in enumerate((
            (dt_hbm, dt_ref), (a_hbm, a_ref), (bias_hbm, bias_ref),
            (x_hbm, x_ref), (b_hbm.at[:, lanes], b_ref), (s0_hbm, s0_ref),
        ))
    ]
    for copy in copies:
        copy.start()
    row = lax.broadcasted_iota(jnp.int32, (length, length), 0)
    lane = lax.broadcasted_iota(jnp.int32, (length, length), 1)
    upper = jnp.where(row <= lane, 1.0, 0.0).astype(bf16)
    pick_ref[...] = picks(heads, width, 2)
    for copy in copies[:3]:
        copy.wait()
    delta = softplus(dt_ref[...] + as_column(bias_ref[...])) * valid_ref[...]
    rate = delta * as_column(a_ref[...]) * (-LOG2E)
    sums = jnp.dot(
        jnp.concatenate(split(rate, 3), axis=1),
        jnp.concatenate([upper] * 3, axis=0),
        preferred_element_type=f32,
    )
    sums_ref[...] = sums
    delta_ref[...] = delta
    last = sums[:, length - 1 :]
    weight = jnp.exp2(last - sums) * delta
    total = widen_row(jnp.exp2(last), width)
    copies[3].wait()
    copies[4].wait()
    wide = widen_columns(weight, pick_ref)
    xw = (x_ref[...].astype(f32) * wide).astype(bf16)
    fresh = lax.dot_general(b_ref[...], xw, (((0,), (0,)), ((), ())), preferred_element_type=f32)
    fresh_ref[...] = fresh
    copies[5].wait()
    for i in range(16):
        rows = slice(i * states // 16, (i + 1) * states // 16)
        fs_ref[rows, :] = (fresh_ref[rows, :] + total * s0_ref[rows, :]).astype(bf16)


def read_kernel(fs_ref, query_ref, out_ref):
    states, width = fs_ref.shape
    me = lax.axis_index("sample")
    block = query_ref[:, group_lanes(states, width // 64)].astype(f32)
    mine = lax.broadcasted_iota(jnp.int32, block.shape, 0) == me
    query = jnp.sum(jnp.where(mine, block, 0.0), axis=0, keepdims=True).astype(bf16)
    out_ref[...] = jnp.dot(query, fs_ref[...], preferred_element_type=f32)


def prompt_kernel(
    fs_ref, x_ref, z_ref, b_ref, cp_ref, s0_ref, sums_ref, delta_ref, skip_ref, gain_ref,
    xd_ref, zd_ref, bd_ref, cd_ref, dtd_ref, a_ref, bias_ref,
    gated_ref, sq_ref, u_ref, v_ref, own_ref, fs_hbm, m_ref, sem,
):
    heads, length = sums_ref.shape
    states, width = s0_ref.shape
    per = width // heads
    prompts = xd_ref.shape[0]
    store = pltpu.make_async_copy(fs_ref, fs_hbm, sem)
    store.start()
    lanes = group_lanes(states, heads)
    cp = cp_ref[:, lanes]
    scores = lax.dot_general(cp, b_ref[...], (((1,), (1,)), ((), ())), preferred_element_type=f32)
    row = lax.broadcasted_iota(jnp.int32, (length, length), 0)
    lane = lax.broadcasted_iota(jnp.int32, (length, length), 1)
    scores = jnp.where(row >= lane, scores, 0.0)
    m_ref[...] = jnp.dot(cp, s0_ref[...].astype(bf16), preferred_element_type=f32)

    step = softplus(dtd_ref[...] + bias_ref[...])
    own = cd_ref[:, lanes].astype(f32)
    cb = own * bd_ref[:, lanes].astype(f32)
    cb = jnp.sum(cb, axis=1, keepdims=True)
    gain = step * cb + skip_ref[...]
    skips = jnp.broadcast_to(skip_ref[...], (8, heads))
    wide = widen(jnp.concatenate([jnp.exp(-step * a_ref[...]), gain], axis=0), width, 3)
    skip = widen(skips, width, 3)[0:1, :]
    gate = silu(zd_ref[...].astype(f32))
    u_ref[...] = wide[:prompts] * gate
    v_ref[...] = wide[prompts:] * xd_ref[...].astype(f32) * gate

    mine = lax.broadcasted_iota(jnp.int32, own.shape, 0) == lax.axis_index("sample")
    query = jnp.where(mine, own, 0.0)
    query = jnp.sum(query, axis=0, keepdims=True).astype(bf16)
    own_ref[...] = jnp.dot(query, fs_ref[...], preferred_element_type=f32)

    rt = jnp.log2(delta_ref[...]) - sums_ref[...]
    c = sums_ref[...].T
    pair = 2 * per
    low = lax.broadcasted_iota(jnp.int32, (length, pair), 1) < per
    squares = jnp.zeros((length, pair), f32)
    for q in range(heads // 2):
        ch = slice(q * pair, (q + 1) * pair)
        x = x_ref[:, ch]
        xf = x.astype(f32)
        x_cat = jnp.concatenate(
            [jnp.where(low, xf, 0.0).astype(bf16), jnp.where(low, 0.0, xf).astype(bf16)], axis=0
        )
        parts = []
        cols = []
        for h in (2 * q, 2 * q + 1):
            col = jnp.broadcast_to(c[:, h : h + 1], (length, length))
            arg = jnp.minimum(col + rt[h : h + 1, :], CAP)
            parts.append((jnp.exp2(arg) * scores).astype(bf16))
            cols.append(col)
        y = jnp.dot(jnp.concatenate(parts, axis=1), x_cat, preferred_element_type=f32)
        decay = jnp.exp2(jnp.where(low, cols[0], cols[1]))
        y = y + decay * m_ref[:, ch] + skip[:, ch] * xf
        gated = y * silu(z_ref[:, ch].astype(f32))
        gated_ref[:, ch] = gated * gain_ref[:, ch]
        squares = squares + gated * gated
    total = jnp.broadcast_to(jnp.sum(squares, axis=1, keepdims=True), (length, length))
    sq_ref[...] = total.T[0:1, :]
    store.wait()


def slot_kernel(*refs):
    sq_ref, u_ref, v_ref = refs[:3]
    read_refs = refs[3:-2]
    gated_ref, pay_ref = refs[-2:]
    prompts, width = u_ref.shape
    me = lax.axis_index("sample")
    prompt = lax.broadcasted_iota(jnp.int32, (prompts, width), 0)
    reads = jnp.zeros((prompts, width), f32)
    for k, ref in zip([0] + shifts(prompts), read_refs):
        reads = jnp.where(prompt == lax.rem(me + k, prompts), ref[...], reads)
    gated = u_ref[...] * reads + v_ref[...]
    gated_ref[...] = gated
    total = jnp.broadcast_to(jnp.sum(gated * gated, axis=1, keepdims=True), (prompts, 128))
    row = lax.broadcasted_iota(jnp.int32, (prompts, 128), 0)
    lane = lax.broadcasted_iota(jnp.int32, (prompts, 128), 1)
    pay_ref[0:1, :] = sq_ref[...]
    pay_ref[1:2, :] = jnp.sum(jnp.where(row == lane, total, 0.0), axis=0, keepdims=True)


def norm_kernel(*refs, channels, payloads):
    valid_ref, gated_ref, dec_ref, gain_ref = refs[:4]
    pay_refs = refs[4 : 4 + payloads]
    out_hbm, dec_hbm, out_ref, out_dec_ref, sems = refs[4 + payloads :]
    length = gated_ref.shape[0]
    prompts = dec_ref.shape[0]
    total = pay_refs[0][...]
    for ref in pay_refs[1:]:
        total = total + ref[...]
    scale = lax.rsqrt(total * (1.0 / channels) + epsilon)
    row = lax.broadcasted_iota(jnp.int32, (prompts, 128), 0)
    lane = lax.broadcasted_iota(jnp.int32, (prompts, 128), 1)
    wide = jnp.broadcast_to(scale[1:2, :], (prompts, 128))
    dec = jnp.sum(jnp.where(row == lane, wide, 0.0), axis=1, keepdims=True)
    out_dec_ref[...] = (dec_ref[...] * dec * gain_ref[...]).astype(bf16)
    copies = [pltpu.make_async_copy(out_dec_ref, dec_hbm, sems.at[0])]
    copies[0].start()
    column = jnp.broadcast_to(scale[0:1, :] * valid_ref[...], (length, length)).T[:, 0:1]
    for i in range(CHUNKS):
        rows = slice(i * length // CHUNKS, (i + 1) * length // CHUNKS)
        out_ref[rows, :] = (gated_ref[rows, :] * column[rows, :]).astype(bf16)
        copies.append(
            pltpu.make_async_copy(out_ref.at[rows, :], out_hbm.at[rows, :], sems.at[1 + i])
        )
        copies[-1].start()
    for copy in copies:
        copy.wait()


VMEM = pltpu.MemorySpace.VMEM
HBM = pltpu.MemorySpace.HBM


def call(kernel, ins, outs, scratch=(), far=(), fetch=False):
    spaces = [VMEM if not fetch or i == 0 else HBM for i in range(len(ins))]
    outs = [(VMEM, *out) for out in outs] + [(HBM, *out) for out in far]
    return pl.pallas_call(
        kernel,
        in_specs=[pl.BlockSpec(memory_space=space) for space in spaces],
        out_specs=tuple(pl.BlockSpec(memory_space=out[0]) for out in outs),
        out_shape=tuple(out[0](*out[1:]) for out in outs),
        scratch_shapes=list(scratch),
        compiler_params=pltpu.CompilerParams(vmem_limit_bytes=GRANT),
    )(*(pltpu.with_memory_space_constraint(v, space) for v, space in zip(ins, spaces)))


def shifts(n):
    return [k for j in range(1, n // 2 + 1) for k in dict.fromkeys((j, n - j))]


def make_body(mesh):
    samples = mesh.shape["sample"]
    head_parts = mesh.shape["head"]

    def body(
        x_pre, z_pre, b_pre, c_pre, dt_pre, lengths, init_state, a_rates, dt_bias, skip_scale,
        norm_gain, x_dec, z_dec, b_dec, c_dec, dt_dec,
    ):
        return layer(
            x_pre, z_pre, b_pre, c_pre, dt_pre, lengths, init_state, a_rates, dt_bias,
            skip_scale, norm_gain, x_dec, z_dec, b_dec, c_dec, dt_dec,
        )

    def layer(
        x_pre, z_pre, b_pre, c_pre, dt_pre, lengths, init_state, a_rates, dt_bias, skip_scale,
        norm_gain, x_dec, z_dec, b_dec, c_dec, dt_dec,
    ):
        length, width = x_pre.shape[1:]
        states = init_state.shape[1]
        heads = a_rates.shape[0]
        prompts = x_dec.shape[1]
        x, z, b, cp, dt, s0 = (v[0] for v in (x_pre, z_pre, b_pre, c_pre, dt_pre, init_state))
        xd, zd, bd, cd, dtd = (v[0] for v in (x_dec, z_dec, b_dec, c_dec, dt_dec))
        a, bias, skip, gain = (v[None] for v in (a_rates, dt_bias, skip_scale, norm_gain))

        def shifted(v, k):
            pairs = [(j, (j + k) % samples) for j in range(samples)]
            return lax.ppermute(v, "sample", pairs)

        queries = [shifted(cd, k) for k in shifts(samples)]
        positions = jnp.arange(length, dtype=jnp.int32)
        valid = (positions[None, :] < lengths[:, None]).astype(f32)
        fs, sums, delta, x, b, s0, a, bias = call(
            state_kernel, (valid, dt.T, a, bias, x, b, s0),
            (
                ((states, width), bf16), ((heads, length), f32), ((heads, length), f32),
                ((length, width), bf16), ((length, states), bf16), ((states, width), f32),
                ((1, heads), f32), ((1, heads), f32),
            ),
            (
                pltpu.VMEM((heads, length), f32), pltpu.VMEM((2 * heads, width), bf16),
                pltpu.VMEM((states, width), f32),
                pltpu.SemaphoreType.DMA((6,)),
            ), fetch=True,
        )
        reads = []
        for k, query in zip(shifts(samples), queries):
            (answer,) = call(read_kernel, (fs, query), (((1, width), f32),))
            reads.append(shifted(answer, -k))
        gated, sq, u, v, mine, fs = call(
            prompt_kernel,
            (fs, x, z, b, cp, s0, sums, delta, skip, gain, xd, zd, bd, cd, dtd, a, bias),
            (((length, width), f32), ((1, length), f32)) + (((prompts, width), f32),) * 2
            + (((1, width), f32),),
            (pltpu.VMEM((length, width), f32), pltpu.SemaphoreType.DMA(())),
            (((states, width), bf16),),
        )
        gated_dec, pay = call(
            slot_kernel, (sq, u, v, mine, *reads),
            (((prompts, width), f32), ((2, 128), f32)),
        )
        pays = [pay] + [
            lax.ppermute(pay, "head", [(j, j ^ k) for j in range(head_parts)])
            for k in range(head_parts - 1, 0, -1)
        ]
        out_pre, out_dec = call(
            functools.partial(norm_kernel, channels=width * head_parts, payloads=head_parts),
            (valid, gated, gated_dec, gain, *pays), (),
            (
                pltpu.VMEM((length, width), bf16), pltpu.VMEM((prompts, width), bf16),
                pltpu.SemaphoreType.DMA((1 + CHUNKS,)),
            ), (((length, width), bf16), ((prompts, width), bf16)),
        )
        return out_pre[None], fs[None], out_dec[None]

    return body


def solution(mesh):
    tokens = P(("rep", "sample"), None, "head")
    groups = P(("rep", "sample"), None, None)
    in_specs = (
        tokens, tokens, groups, groups, tokens, P(("rep", "sample")), tokens,
        P("head"), P("head"), P("head"), P("head"), tokens, tokens, groups, groups, tokens,
    )
    return jax.shard_map(
        make_body(mesh), mesh=mesh, in_specs=in_specs, out_specs=(tokens,) * 3, check_vma=False
    )
```

```python
import functools

import jax
import jax.numpy as jnp
from jax import lax
from jax.experimental import pallas as pl
from jax.experimental.pallas import tpu as pltpu
from jax.sharding import PartitionSpec as P


H = 128
G = 4
epsilon = 1e-05
f32 = jnp.float32
bf16 = jnp.bfloat16
LOG2E = 1.4426950408889634
CAP = 100.0
CHUNKS = 4
GRANT = 16 << 20


def softplus(v):
    return jnp.maximum(v, 0.0) + jnp.log1p(jnp.exp(-jnp.abs(v)))


def silu(z):
    half = 0.5 * z
    return half * (1.0 + jnp.tanh(half))


def split(v, parts):
    out = []
    for _ in range(parts):
        piece = v.astype(bf16)
        out.append(piece)
        v = v - piece.astype(f32)
    return out


def picks(heads, width, parts):
    per = width // heads
    row = lax.broadcasted_iota(jnp.int32, (heads, width), 0)
    lane = lax.broadcasted_iota(jnp.int32, (heads, width), 1)
    pick = jnp.where((lane >= row * per) & (lane < (row + 1) * per), 1.0, 0.0).astype(bf16)
    return jnp.concatenate([pick] * parts, axis=0)


def widen(v, width, parts):
    lhs = jnp.concatenate(split(v, parts), axis=1)
    return jnp.dot(lhs, picks(v.shape[1], width, parts), preferred_element_type=f32)


def as_column(row):
    n = row.shape[1]
    wide = jnp.broadcast_to(row, (n, n))
    here = lax.broadcasted_iota(jnp.int32, (n, n), 0) == lax.broadcasted_iota(jnp.int32, (n, n), 1)
    return jnp.sum(jnp.where(here, wide, 0.0), axis=1, keepdims=True)


def widen_columns(v, pick_ref):
    lhs = jnp.concatenate(split(v, pick_ref.shape[0] // v.shape[0]), axis=0)
    return lax.dot_general(
        lhs, pick_ref[...], (((0,), (0,)), ((), ())), preferred_element_type=f32
    )


def widen_row(v, width):
    heads = v.shape[0]
    per = width // heads
    wide = jnp.broadcast_to(v, (heads, 2 * per))
    low = lax.broadcasted_iota(jnp.int32, (1, 2 * per), 1) < per
    rows = [jnp.where(low, wide[i : i + 1], wide[i + 1 : i + 2]) for i in range(0, heads, 2)]
    return jnp.concatenate(rows, axis=1)


def group_lanes(states, heads_here):
    start = (lax.axis_index("head") * heads_here) // (H // G)
    return pl.ds(pl.multiple_of(start * states, states), states)


def state_kernel(
    valid_ref, dt_hbm, a_hbm, bias_hbm, x_hbm, b_hbm, s0_hbm,
    fs_ref, sums_ref, delta_ref, x_ref, b_ref, s0_ref, a_ref, bias_ref,
    dt_ref, pick_ref, fresh_ref, sems,
):
    heads, length = dt_ref.shape
    width = x_ref.shape[1]
    states = s0_ref.shape[0]
    lanes = group_lanes(states, heads)
    copies = [
        pltpu.make_async_copy(source, target, sems.at[i])
        for i, (source, target) in enumerate((
            (dt_hbm, dt_ref), (a_hbm, a_ref), (bias_hbm, bias_ref),
            (x_hbm, x_ref), (b_hbm.at[:, lanes], b_ref), (s0_hbm, s0_ref),
        ))
    ]
    for copy in copies:
        copy.start()
    row = lax.broadcasted_iota(jnp.int32, (length, length), 0)
    lane = lax.broadcasted_iota(jnp.int32, (length, length), 1)
    upper = jnp.where(row <= lane, 1.0, 0.0).astype(bf16)
    pick_ref[...] = picks(heads, width, 2)
    for copy in copies[:3]:
        copy.wait()
    delta = softplus(dt_ref[...] + as_column(bias_ref[...])) * valid_ref[...]
    rate = delta * as_column(a_ref[...]) * (-LOG2E)
    sums = jnp.dot(
        jnp.concatenate(split(rate, 3), axis=1),
        jnp.concatenate([upper] * 3, axis=0),
        preferred_element_type=f32,
    )
    sums_ref[...] = sums
    delta_ref[...] = delta
    last = sums[:, length - 1 :]
    weight = jnp.exp2(last - sums) * delta
    total = widen_row(jnp.exp2(last), width)
    copies[3].wait()
    copies[4].wait()
    wide = widen_columns(weight, pick_ref)
    xw = (x_ref[...].astype(f32) * wide).astype(bf16)
    fresh = lax.dot_general(b_ref[...], xw, (((0,), (0,)), ((), ())), preferred_element_type=f32)
    fresh_ref[...] = fresh
    copies[5].wait()
    for i in range(16):
        rows = slice(i * states // 16, (i + 1) * states // 16)
        fs_ref[rows, :] = (fresh_ref[rows, :] + total * s0_ref[rows, :]).astype(bf16)


def read_kernel(fs_ref, query_ref, out_ref):
    states, width = fs_ref.shape
    me = lax.axis_index("sample")
    block = query_ref[:, group_lanes(states, width // 64)].astype(f32)
    mine = lax.broadcasted_iota(jnp.int32, block.shape, 0) == me
    query = jnp.sum(jnp.where(mine, block, 0.0), axis=0, keepdims=True).astype(bf16)
    reads = jnp.dot(query, fs_ref[...], preferred_element_type=f32)
    rows = [reads[:, i * 128 : (i + 1) * 128] for i in range(width // 128)]
    out_ref[...] = jnp.concatenate(rows, axis=0).astype(bf16)


def prompt_kernel(
    fs_ref, x_ref, z_ref, b_ref, cp_ref, s0_ref, sums_ref, delta_ref, skip_ref, gain_ref,
    xd_ref, zd_ref, bd_ref, cd_ref, dtd_ref, a_ref, bias_ref,
    gated_ref, sq_ref, u_ref, v_ref, own_ref, fs_hbm, m_ref, sem,
):
    heads, length = sums_ref.shape
    states, width = s0_ref.shape
    per = width // heads
    prompts = xd_ref.shape[0]
    store = pltpu.make_async_copy(fs_ref, fs_hbm, sem)
    store.start()
    lanes = group_lanes(states, heads)
    cp = cp_ref[:, lanes]
    scores = lax.dot_general(cp, b_ref[...], (((1,), (1,)), ((), ())), preferred_element_type=f32)
    row = lax.broadcasted_iota(jnp.int32, (length, length), 0)
    lane = lax.broadcasted_iota(jnp.int32, (length, length), 1)
    scores = jnp.where(row >= lane, scores, 0.0)
    m_ref[...] = jnp.dot(cp, s0_ref[...].astype(bf16), preferred_element_type=f32)

    step = softplus(dtd_ref[...] + bias_ref[...])
    own = cd_ref[:, lanes].astype(f32)
    cb = own * bd_ref[:, lanes].astype(f32)
    cb = jnp.sum(cb, axis=1, keepdims=True)
    gain = step * cb + skip_ref[...]
    skips = jnp.broadcast_to(skip_ref[...], (8, heads))
    wide = widen(jnp.concatenate([jnp.exp(-step * a_ref[...]), gain], axis=0), width, 3)
    skip = widen(skips, width, 3)[0:1, :]
    gate = silu(zd_ref[...].astype(f32))
    u_ref[...] = wide[:prompts] * gate
    v_ref[...] = wide[prompts:] * xd_ref[...].astype(f32) * gate

    mine = lax.broadcasted_iota(jnp.int32, own.shape, 0) == lax.axis_index("sample")
    query = jnp.where(mine, own, 0.0)
    query = jnp.sum(query, axis=0, keepdims=True).astype(bf16)
    own_ref[...] = jnp.dot(query, fs_ref[...], preferred_element_type=f32)

    rt = jnp.log2(delta_ref[...]) - sums_ref[...]
    c = sums_ref[...].T
    pair = 2 * per
    low = lax.broadcasted_iota(jnp.int32, (length, pair), 1) < per
    squares = jnp.zeros((length, pair), f32)
    for q in range(heads // 2):
        ch = slice(q * pair, (q + 1) * pair)
        x = x_ref[:, ch]
        xf = x.astype(f32)
        x_cat = jnp.concatenate(
            [jnp.where(low, xf, 0.0).astype(bf16), jnp.where(low, 0.0, xf).astype(bf16)], axis=0
        )
        parts = []
        cols = []
        for h in (2 * q, 2 * q + 1):
            col = jnp.broadcast_to(c[:, h : h + 1], (length, length))
            arg = jnp.minimum(col + rt[h : h + 1, :], CAP)
            parts.append((jnp.exp2(arg) * scores).astype(bf16))
            cols.append(col)
        y = jnp.dot(jnp.concatenate(parts, axis=1), x_cat, preferred_element_type=f32)
        decay = jnp.exp2(jnp.where(low, cols[0], cols[1]))
        y = y + decay * m_ref[:, ch] + skip[:, ch] * xf
        gated = y * silu(z_ref[:, ch].astype(f32))
        gated_ref[:, ch] = gated * gain_ref[:, ch]
        squares = squares + gated * gated
    total = jnp.broadcast_to(jnp.sum(squares, axis=1, keepdims=True), (length, length))
    sq_ref[...] = total.T[0:1, :]
    store.wait()


def slot_kernel(*refs):
    sq_ref, u_ref, v_ref = refs[:3]
    read_refs = refs[3:-2]
    gated_ref, pay_ref = refs[-2:]
    prompts, width = u_ref.shape
    me = lax.axis_index("sample")
    prompt = lax.broadcasted_iota(jnp.int32, (prompts, width), 0)
    reads = jnp.zeros((prompts, width), f32)
    for k, ref in zip([0] + shifts(prompts), read_refs):
        answer = ref[...].astype(f32)
        if k:
            answer = jnp.concatenate([answer[i : i + 1] for i in range(width // 128)], axis=1)
        reads = jnp.where(prompt == lax.rem(me + k, prompts), answer, reads)
    gated = u_ref[...] * reads + v_ref[...]
    gated_ref[...] = gated
    total = jnp.broadcast_to(jnp.sum(gated * gated, axis=1, keepdims=True), (prompts, 128))
    row = lax.broadcasted_iota(jnp.int32, (prompts, 128), 0)
    lane = lax.broadcasted_iota(jnp.int32, (prompts, 128), 1)
    pay_ref[0:1, :] = sq_ref[...]
    pay_ref[1:2, :] = jnp.sum(jnp.where(row == lane, total, 0.0), axis=0, keepdims=True)


def norm_kernel(*refs, channels, payloads):
    valid_ref, gated_ref, dec_ref, gain_ref = refs[:4]
    pay_refs = refs[4 : 4 + payloads]
    out_hbm, dec_hbm, out_ref, out_dec_ref, sems = refs[4 + payloads :]
    length = gated_ref.shape[0]
    prompts = dec_ref.shape[0]
    total = pay_refs[0][...]
    for ref in pay_refs[1:]:
        total = total + ref[...]
    scale = lax.rsqrt(total * (1.0 / channels) + epsilon)
    row = lax.broadcasted_iota(jnp.int32, (prompts, 128), 0)
    lane = lax.broadcasted_iota(jnp.int32, (prompts, 128), 1)
    wide = jnp.broadcast_to(scale[1:2, :], (prompts, 128))
    dec = jnp.sum(jnp.where(row == lane, wide, 0.0), axis=1, keepdims=True)
    out_dec_ref[...] = (dec_ref[...] * dec * gain_ref[...]).astype(bf16)
    copies = [pltpu.make_async_copy(out_dec_ref, dec_hbm, sems.at[0])]
    copies[0].start()
    column = jnp.broadcast_to(scale[0:1, :] * valid_ref[...], (length, length)).T[:, 0:1]
    for i in range(CHUNKS):
        rows = slice(i * length // CHUNKS, (i + 1) * length // CHUNKS)
        out_ref[rows, :] = (gated_ref[rows, :] * column[rows, :]).astype(bf16)
        copies.append(
            pltpu.make_async_copy(out_ref.at[rows, :], out_hbm.at[rows, :], sems.at[1 + i])
        )
        copies[-1].start()
    for copy in copies:
        copy.wait()


VMEM = pltpu.MemorySpace.VMEM
HBM = pltpu.MemorySpace.HBM


def call(kernel, ins, outs, scratch=(), far=(), fetch=False):
    spaces = [VMEM if not fetch or i == 0 else HBM for i in range(len(ins))]
    outs = [(VMEM, *out) for out in outs] + [(HBM, *out) for out in far]
    return pl.pallas_call(
        kernel,
        in_specs=[pl.BlockSpec(memory_space=space) for space in spaces],
        out_specs=tuple(pl.BlockSpec(memory_space=out[0]) for out in outs),
        out_shape=tuple(out[0](*out[1:]) for out in outs),
        scratch_shapes=list(scratch),
        compiler_params=pltpu.CompilerParams(vmem_limit_bytes=GRANT),
    )(*(pltpu.with_memory_space_constraint(v, space) for v, space in zip(ins, spaces)))


def shifts(n):
    return [k for j in range(1, n // 2 + 1) for k in dict.fromkeys((j, n - j))]


def make_body(mesh):
    samples = mesh.shape["sample"]
    head_parts = mesh.shape["head"]

    def body(
        x_pre, z_pre, b_pre, c_pre, dt_pre, lengths, init_state, a_rates, dt_bias, skip_scale,
        norm_gain, x_dec, z_dec, b_dec, c_dec, dt_dec,
    ):
        return layer(
            x_pre, z_pre, b_pre, c_pre, dt_pre, lengths, init_state, a_rates, dt_bias,
            skip_scale, norm_gain, x_dec, z_dec, b_dec, c_dec, dt_dec,
        )

    def layer(
        x_pre, z_pre, b_pre, c_pre, dt_pre, lengths, init_state, a_rates, dt_bias, skip_scale,
        norm_gain, x_dec, z_dec, b_dec, c_dec, dt_dec,
    ):
        length, width = x_pre.shape[1:]
        states = init_state.shape[1]
        heads = a_rates.shape[0]
        prompts = x_dec.shape[1]
        x, z, b, cp, dt, s0 = (v[0] for v in (x_pre, z_pre, b_pre, c_pre, dt_pre, init_state))
        xd, zd, bd, cd, dtd = (v[0] for v in (x_dec, z_dec, b_dec, c_dec, dt_dec))
        a, bias, skip, gain = (v[None] for v in (a_rates, dt_bias, skip_scale, norm_gain))

        def shifted(v, k):
            pairs = [(j, (j + k) % samples) for j in range(samples)]
            return lax.ppermute(v, "sample", pairs)

        queries = [shifted(cd, k) for k in shifts(samples)]
        positions = jnp.arange(length, dtype=jnp.int32)
        valid = (positions[None, :] < lengths[:, None]).astype(f32)
        fs, sums, delta, x, b, s0, a, bias = call(
            state_kernel, (valid, dt.T, a, bias, x, b, s0),
            (
                ((states, width), bf16), ((heads, length), f32), ((heads, length), f32),
                ((length, width), bf16), ((length, states), bf16), ((states, width), f32),
                ((1, heads), f32), ((1, heads), f32),
            ),
            (
                pltpu.VMEM((heads, length), f32), pltpu.VMEM((2 * heads, width), bf16),
                pltpu.VMEM((states, width), f32),
                pltpu.SemaphoreType.DMA((6,)),
            ), fetch=True,
        )
        reads = []
        for k, query in zip(shifts(samples), queries):
            (answer,) = call(read_kernel, (fs, query), (((width // 128, 128), bf16),))
            reads.append(shifted(answer, -k))
        gated, sq, u, v, mine, fs = call(
            prompt_kernel,
            (fs, x, z, b, cp, s0, sums, delta, skip, gain, xd, zd, bd, cd, dtd, a, bias),
            (((length, width), f32), ((1, length), f32)) + (((prompts, width), f32),) * 2
            + (((1, width), f32),),
            (pltpu.VMEM((length, width), f32), pltpu.SemaphoreType.DMA(())),
            (((states, width), bf16),),
        )
        gated_dec, pay = call(
            slot_kernel, (sq, u, v, mine, *reads),
            (((prompts, width), f32), ((2, 128), f32)),
        )
        pays = [pay] + [
            lax.ppermute(pay, "head", [(j, j ^ k) for j in range(head_parts)])
            for k in range(head_parts - 1, 0, -1)
        ]
        out_pre, out_dec = call(
            functools.partial(norm_kernel, channels=width * head_parts, payloads=head_parts),
            (valid, gated, gated_dec, gain, *pays), (),
            (
                pltpu.VMEM((length, width), bf16), pltpu.VMEM((prompts, width), bf16),
                pltpu.SemaphoreType.DMA((1 + CHUNKS,)),
            ), (((length, width), bf16), ((prompts, width), bf16)),
        )
        return out_pre[None], fs[None], out_dec[None]

    return body


def solution(mesh):
    tokens = P(("rep", "sample"), None, "head")
    groups = P(("rep", "sample"), None, None)
    in_specs = (
        tokens, tokens, groups, groups, tokens, P(("rep", "sample")), tokens,
        P("head"), P("head"), P("head"), P("head"), tokens, tokens, groups, groups, tokens,
    )
    return jax.shard_map(
        make_body(mesh), mesh=mesh, in_specs=in_specs, out_specs=(tokens,) * 3, check_vma=False
    )
```

```python
import functools

import jax
import jax.numpy as jnp
from jax import lax
from jax.experimental import pallas as pl
from jax.experimental.pallas import tpu as pltpu
from jax.sharding import PartitionSpec as P


H = 128
G = 4
epsilon = 1e-05
f32 = jnp.float32
bf16 = jnp.bfloat16
LOG2E = 1.4426950408889634
CAP = 100.0
CHUNKS = 4
GRANT = 16 << 20


def softplus(v):
    return jnp.maximum(v, 0.0) + jnp.log1p(jnp.exp(-jnp.abs(v)))


def silu(z):
    half = 0.5 * z
    return half * (1.0 + jnp.tanh(half))


def split(v, parts):
    out = []
    for _ in range(parts):
        piece = v.astype(bf16)
        out.append(piece)
        v = v - piece.astype(f32)
    return out


def picks(heads, width, parts):
    per = width // heads
    row = lax.broadcasted_iota(jnp.int32, (heads, width), 0)
    lane = lax.broadcasted_iota(jnp.int32, (heads, width), 1)
    pick = jnp.where((lane >= row * per) & (lane < (row + 1) * per), 1.0, 0.0).astype(bf16)
    return jnp.concatenate([pick] * parts, axis=0)


def widen(v, width, parts):
    lhs = jnp.concatenate(split(v, parts), axis=1)
    return jnp.dot(lhs, picks(v.shape[1], width, parts), preferred_element_type=f32)


def as_column(row):
    n = row.shape[1]
    wide = jnp.broadcast_to(row, (n, n))
    here = lax.broadcasted_iota(jnp.int32, (n, n), 0) == lax.broadcasted_iota(jnp.int32, (n, n), 1)
    return jnp.sum(jnp.where(here, wide, 0.0), axis=1, keepdims=True)


def widen_columns(v, pick_ref):
    lhs = jnp.concatenate(split(v, pick_ref.shape[0] // v.shape[0]), axis=0)
    return lax.dot_general(
        lhs, pick_ref[...], (((0,), (0,)), ((), ())), preferred_element_type=f32
    )


def widen_row(v, width):
    heads = v.shape[0]
    per = width // heads
    wide = jnp.broadcast_to(v, (heads, 2 * per))
    low = lax.broadcasted_iota(jnp.int32, (1, 2 * per), 1) < per
    rows = [jnp.where(low, wide[i : i + 1], wide[i + 1 : i + 2]) for i in range(0, heads, 2)]
    return jnp.concatenate(rows, axis=1)


def group_lanes(states, heads_here):
    start = (lax.axis_index("head") * heads_here) // (H // G)
    return pl.ds(pl.multiple_of(start * states, states), states)


def state_kernel(
    valid_ref, dt_hbm, a_hbm, bias_hbm, x_hbm, b_hbm, s0_hbm,
    fs_ref, sums_ref, delta_ref, x_ref, b_ref, s0_ref, a_ref, bias_ref,
    dt_ref, pick_ref, fresh_ref, sems,
):
    heads, length = dt_ref.shape
    width = x_ref.shape[1]
    states = s0_ref.shape[0]
    lanes = group_lanes(states, heads)
    copies = [
        pltpu.make_async_copy(source, target, sems.at[i])
        for i, (source, target) in enumerate((
            (dt_hbm, dt_ref), (a_hbm, a_ref), (bias_hbm, bias_ref),
            (x_hbm, x_ref), (b_hbm.at[:, lanes], b_ref), (s0_hbm, s0_ref),
        ))
    ]
    for copy in copies:
        copy.start()
    row = lax.broadcasted_iota(jnp.int32, (length, length), 0)
    lane = lax.broadcasted_iota(jnp.int32, (length, length), 1)
    upper = jnp.where(row <= lane, 1.0, 0.0).astype(bf16)
    pick_ref[...] = picks(heads, width, 2)
    for copy in copies[:3]:
        copy.wait()
    delta = softplus(dt_ref[...] + as_column(bias_ref[...])) * valid_ref[...]
    rate = delta * as_column(a_ref[...]) * (-LOG2E)
    sums = jnp.dot(
        jnp.concatenate(split(rate, 3), axis=1),
        jnp.concatenate([upper] * 3, axis=0),
        preferred_element_type=f32,
    )
    sums_ref[...] = sums
    delta_ref[...] = delta
    last = sums[:, length - 1 :]
    weight = jnp.exp2(last - sums) * delta
    total = widen_row(jnp.exp2(last), width)
    copies[3].wait()
    copies[4].wait()
    wide = widen_columns(weight, pick_ref)
    xw = (x_ref[...].astype(f32) * wide).astype(bf16)
    fresh = lax.dot_general(b_ref[...], xw, (((0,), (0,)), ((), ())), preferred_element_type=f32)
    fresh_ref[...] = fresh
    copies[5].wait()
    for i in range(16):
        rows = slice(i * states // 16, (i + 1) * states // 16)
        fs_ref[rows, :] = (fresh_ref[rows, :] + total * s0_ref[rows, :]).astype(bf16)


def read_kernel(fs_ref, *refs):
    count = len(refs) // 2
    states, width = fs_ref.shape
    me = lax.axis_index("sample")
    lanes = group_lanes(states, width // 64)
    queries = []
    for query_ref in refs[:count]:
        block = query_ref[:, lanes].astype(f32)
        mine = lax.broadcasted_iota(jnp.int32, block.shape, 0) == me
        queries.append(jnp.sum(jnp.where(mine, block, 0.0), axis=0, keepdims=True))
    query = jnp.concatenate(queries, axis=0).astype(bf16)
    reads = jnp.dot(query, fs_ref[...], preferred_element_type=f32)
    for k, out_ref in enumerate(refs[count:]):
        rows = [reads[k : k + 1, i * 128 : (i + 1) * 128] for i in range(width // 128)]
        out_ref[...] = jnp.concatenate(rows, axis=0).astype(bf16)


def prompt_kernel(
    fs_ref, x_ref, z_ref, b_ref, cp_ref, s0_ref, sums_ref, delta_ref, skip_ref, gain_ref,
    xd_ref, zd_ref, bd_ref, cd_ref, dtd_ref, a_ref, bias_ref,
    gated_ref, sq_ref, u_ref, v_ref, own_ref, fs_hbm, m_ref, sem,
):
    heads, length = sums_ref.shape
    states, width = s0_ref.shape
    per = width // heads
    prompts = xd_ref.shape[0]
    store = pltpu.make_async_copy(fs_ref, fs_hbm, sem)
    store.start()
    lanes = group_lanes(states, heads)
    cp = cp_ref[:, lanes]
    scores = lax.dot_general(cp, b_ref[...], (((1,), (1,)), ((), ())), preferred_element_type=f32)
    row = lax.broadcasted_iota(jnp.int32, (length, length), 0)
    lane = lax.broadcasted_iota(jnp.int32, (length, length), 1)
    scores = jnp.where(row >= lane, scores, 0.0)
    m_ref[...] = jnp.dot(cp, s0_ref[...].astype(bf16), preferred_element_type=f32)

    step = softplus(dtd_ref[...] + bias_ref[...])
    own = cd_ref[:, lanes].astype(f32)
    cb = own * bd_ref[:, lanes].astype(f32)
    cb = jnp.sum(cb, axis=1, keepdims=True)
    gain = step * cb + skip_ref[...]
    skips = jnp.broadcast_to(skip_ref[...], (8, heads))
    wide = widen(jnp.concatenate([jnp.exp(-step * a_ref[...]), gain], axis=0), width, 3)
    skip = widen(skips, width, 3)[0:1, :]
    gate = silu(zd_ref[...].astype(f32))
    u_ref[...] = wide[:prompts] * gate
    v_ref[...] = wide[prompts:] * xd_ref[...].astype(f32) * gate

    mine = lax.broadcasted_iota(jnp.int32, own.shape, 0) == lax.axis_index("sample")
    query = jnp.where(mine, own, 0.0)
    query = jnp.sum(query, axis=0, keepdims=True).astype(bf16)
    own_ref[...] = jnp.dot(query, fs_ref[...], preferred_element_type=f32)

    rt = jnp.log2(delta_ref[...]) - sums_ref[...]
    c = sums_ref[...].T
    pair = 2 * per
    low = lax.broadcasted_iota(jnp.int32, (length, pair), 1) < per
    squares = jnp.zeros((length, pair), f32)
    for q in range(heads // 2):
        ch = slice(q * pair, (q + 1) * pair)
        x = x_ref[:, ch]
        xf = x.astype(f32)
        x_cat = jnp.concatenate(
            [jnp.where(low, xf, 0.0).astype(bf16), jnp.where(low, 0.0, xf).astype(bf16)], axis=0
        )
        parts = []
        cols = []
        for h in (2 * q, 2 * q + 1):
            col = jnp.broadcast_to(c[:, h : h + 1], (length, length))
            arg = jnp.minimum(col + rt[h : h + 1, :], CAP)
            parts.append((jnp.exp2(arg) * scores).astype(bf16))
            cols.append(col)
        y = jnp.dot(jnp.concatenate(parts, axis=1), x_cat, preferred_element_type=f32)
        decay = jnp.exp2(jnp.where(low, cols[0], cols[1]))
        y = y + decay * m_ref[:, ch] + skip[:, ch] * xf
        gated = y * silu(z_ref[:, ch].astype(f32))
        gated_ref[:, ch] = gated * gain_ref[:, ch]
        squares = squares + gated * gated
    total = jnp.broadcast_to(jnp.sum(squares, axis=1, keepdims=True), (length, length))
    sq_ref[...] = total.T[0:1, :]
    store.wait()


def slot_kernel(*refs):
    sq_ref, u_ref, v_ref = refs[:3]
    read_refs = refs[3:-2]
    gated_ref, pay_ref = refs[-2:]
    prompts, width = u_ref.shape
    me = lax.axis_index("sample")
    prompt = lax.broadcasted_iota(jnp.int32, (prompts, width), 0)
    reads = jnp.zeros((prompts, width), f32)
    for k, ref in zip([0] + shifts(prompts), read_refs):
        answer = ref[...].astype(f32)
        if k:
            answer = jnp.concatenate([answer[i : i + 1] for i in range(width // 128)], axis=1)
        reads = jnp.where(prompt == lax.rem(me + k, prompts), answer, reads)
    gated = u_ref[...] * reads + v_ref[...]
    gated_ref[...] = gated
    total = jnp.broadcast_to(jnp.sum(gated * gated, axis=1, keepdims=True), (prompts, 128))
    row = lax.broadcasted_iota(jnp.int32, (prompts, 128), 0)
    lane = lax.broadcasted_iota(jnp.int32, (prompts, 128), 1)
    pay_ref[0:1, :] = sq_ref[...]
    pay_ref[1:2, :] = jnp.sum(jnp.where(row == lane, total, 0.0), axis=0, keepdims=True)


def norm_kernel(*refs, channels, payloads):
    valid_ref, gated_ref, dec_ref, gain_ref = refs[:4]
    pay_refs = refs[4 : 4 + payloads]
    out_hbm, dec_hbm, out_ref, out_dec_ref, sems = refs[4 + payloads :]
    length = gated_ref.shape[0]
    prompts = dec_ref.shape[0]
    total = pay_refs[0][...]
    for ref in pay_refs[1:]:
        total = total + ref[...]
    scale = lax.rsqrt(total * (1.0 / channels) + epsilon)
    row = lax.broadcasted_iota(jnp.int32, (prompts, 128), 0)
    lane = lax.broadcasted_iota(jnp.int32, (prompts, 128), 1)
    wide = jnp.broadcast_to(scale[1:2, :], (prompts, 128))
    dec = jnp.sum(jnp.where(row == lane, wide, 0.0), axis=1, keepdims=True)
    out_dec_ref[...] = (dec_ref[...] * dec * gain_ref[...]).astype(bf16)
    copies = [pltpu.make_async_copy(out_dec_ref, dec_hbm, sems.at[0])]
    copies[0].start()
    column = jnp.broadcast_to(scale[0:1, :] * valid_ref[...], (length, length)).T[:, 0:1]
    for i in range(CHUNKS):
        rows = slice(i * length // CHUNKS, (i + 1) * length // CHUNKS)
        out_ref[rows, :] = (gated_ref[rows, :] * column[rows, :]).astype(bf16)
        copies.append(
            pltpu.make_async_copy(out_ref.at[rows, :], out_hbm.at[rows, :], sems.at[1 + i])
        )
        copies[-1].start()
    for copy in copies:
        copy.wait()


VMEM = pltpu.MemorySpace.VMEM
HBM = pltpu.MemorySpace.HBM


def call(kernel, ins, outs, scratch=(), far=(), fetch=False):
    spaces = [VMEM if not fetch or i == 0 else HBM for i in range(len(ins))]
    outs = [(VMEM, *out) for out in outs] + [(HBM, *out) for out in far]
    return pl.pallas_call(
        kernel,
        in_specs=[pl.BlockSpec(memory_space=space) for space in spaces],
        out_specs=tuple(pl.BlockSpec(memory_space=out[0]) for out in outs),
        out_shape=tuple(out[0](*out[1:]) for out in outs),
        scratch_shapes=list(scratch),
        compiler_params=pltpu.CompilerParams(vmem_limit_bytes=GRANT),
    )(*(pltpu.with_memory_space_constraint(v, space) for v, space in zip(ins, spaces)))


def shifts(n):
    return [k for j in range(1, n // 2 + 1) for k in dict.fromkeys((j, n - j))]


def make_body(mesh):
    samples = mesh.shape["sample"]
    head_parts = mesh.shape["head"]

    def body(
        x_pre, z_pre, b_pre, c_pre, dt_pre, lengths, init_state, a_rates, dt_bias, skip_scale,
        norm_gain, x_dec, z_dec, b_dec, c_dec, dt_dec,
    ):
        return layer(
            x_pre, z_pre, b_pre, c_pre, dt_pre, lengths, init_state, a_rates, dt_bias,
            skip_scale, norm_gain, x_dec, z_dec, b_dec, c_dec, dt_dec,
        )

    def layer(
        x_pre, z_pre, b_pre, c_pre, dt_pre, lengths, init_state, a_rates, dt_bias, skip_scale,
        norm_gain, x_dec, z_dec, b_dec, c_dec, dt_dec,
    ):
        length, width = x_pre.shape[1:]
        states = init_state.shape[1]
        heads = a_rates.shape[0]
        prompts = x_dec.shape[1]
        x, z, b, cp, dt, s0 = (v[0] for v in (x_pre, z_pre, b_pre, c_pre, dt_pre, init_state))
        xd, zd, bd, cd, dtd = (v[0] for v in (x_dec, z_dec, b_dec, c_dec, dt_dec))
        a, bias, skip, gain = (v[None] for v in (a_rates, dt_bias, skip_scale, norm_gain))

        def shifted(v, k):
            pairs = [(j, (j + k) % samples) for j in range(samples)]
            return lax.ppermute(v, "sample", pairs)

        queries = [shifted(cd, k) for k in shifts(samples)]
        positions = jnp.arange(length, dtype=jnp.int32)
        valid = (positions[None, :] < lengths[:, None]).astype(f32)
        fs, sums, delta, x, b, s0, a, bias = call(
            state_kernel, (valid, dt.T, a, bias, x, b, s0),
            (
                ((states, width), bf16), ((heads, length), f32), ((heads, length), f32),
                ((length, width), bf16), ((length, states), bf16), ((states, width), f32),
                ((1, heads), f32), ((1, heads), f32),
            ),
            (
                pltpu.VMEM((heads, length), f32), pltpu.VMEM((2 * heads, width), bf16),
                pltpu.VMEM((states, width), f32),
                pltpu.SemaphoreType.DMA((6,)),
            ), fetch=True,
        )
        reads = []
        answers = []
        for some in (queries[:1], queries[1:]):
            shape = ((width // 128, 128), bf16)
            answers += call(read_kernel, (fs, *some), (shape,) * len(some))
        for k, answer in zip(shifts(samples), answers):
            reads.append(shifted(answer, -k))
        gated, sq, u, v, mine, fs = call(
            prompt_kernel,
            (fs, x, z, b, cp, s0, sums, delta, skip, gain, xd, zd, bd, cd, dtd, a, bias),
            (((length, width), f32), ((1, length), f32)) + (((prompts, width), f32),) * 2
            + (((1, width), f32),),
            (pltpu.VMEM((length, width), f32), pltpu.SemaphoreType.DMA(())),
            (((states, width), bf16),),
        )
        gated_dec, pay = call(
            slot_kernel, (sq, u, v, mine, *reads),
            (((prompts, width), f32), ((2, 128), f32)),
        )
        pays = [pay] + [
            lax.ppermute(pay, "head", [(j, j ^ k) for j in range(head_parts)])
            for k in range(head_parts - 1, 0, -1)
        ]
        out_pre, out_dec = call(
            functools.partial(norm_kernel, channels=width * head_parts, payloads=head_parts),
            (valid, gated, gated_dec, gain, *pays), (),
            (
                pltpu.VMEM((length, width), bf16), pltpu.VMEM((prompts, width), bf16),
                pltpu.SemaphoreType.DMA((1 + CHUNKS,)),
            ), (((length, width), bf16), ((prompts, width), bf16)),
        )
        return out_pre[None], fs[None], out_dec[None]

    return body


def solution(mesh):
    tokens = P(("rep", "sample"), None, "head")
    groups = P(("rep", "sample"), None, None)
    in_specs = (
        tokens, tokens, groups, groups, tokens, P(("rep", "sample")), tokens,
        P("head"), P("head"), P("head"), P("head"), tokens, tokens, groups, groups, tokens,
    )
    return jax.shard_map(
        make_body(mesh), mesh=mesh, in_specs=in_specs, out_specs=(tokens,) * 3, check_vma=False
    )
```
